32 devices in a mesh: section: 16 (over z, y, core), dp: 2 (over x).
Axes of the slice: x: 2, y: 2, z: 4, core: 2. Of those that a mesh axis runs over, the one named last changes fastest.
Arguments:
- activations: bfloat16 [16, 16, 64, 4096], P('section', 'dp'), may hold values from -6 to 6
- out_grads: bfloat16 [16, 16, 64, 4096], P('section', 'dp'), may hold values from -6 to 6
- proj_in: bfloat16 [16, 2, 4096, 128], P('section'), may hold values from -0.09375 to 0.09375
- proj_out: bfloat16 [16, 2, 64, 4096], P('section'), may hold values from -0.09375 to 0.09375
- earlier_gram: float32 [8192, 8192], P('section', 'dp'), may hold values from -4 to 4, as said below
Outputs:
- gram: float32 [8192, 8192], P('section', 'dp')
The draws below stay inside these ranges and needn't reach their ends.
Inputs may be any that keep to these rules, and one draw needn't show every extreme that they name: earlier_gram is symmetric.
All inputs are finite; a program needn't handle non-finite values.
Results may differ from the reference program's by a relative error of at most 0.0013.
Values sent between devices are 32-bit elements; how exact they have to be, the bound alone decides.
A program may use at most 64 MiB of HBM per device.

```python
import math
import jax
import jax.numpy as jnp
from jax import lax

D = 4096
K_IN = 128
K_OUT = 64
PROJ = 2
LEN = 64
LAYERS = 16
EXAMPLES = 16
K = 8192


def draw_earlier_gram(key, part):
    noise = jax.random.normal(jax.random.fold_in(key, 17), (K, K), jnp.float32)
    return jnp.clip((noise + noise.T) * 0.5, -4.0, 4.0)


def steps_of(stream_key, shape, cuts, least, largest):
    gain = 1.0
    for position, parts in cuts:
        heights = jax.random.uniform(jax.random.fold_in(jax.random.fold_in(stream_key, 6), position), (parts,), jnp.float32, least / len(cuts), largest / len(cuts))
        gain = gain * jnp.repeat(jnp.exp(heights), shape[position] // parts).reshape((-1,) + (1,) * (len(shape) - 1 - position))
    return gain


def centred(rng, shape, deviation, most, shards=(), kind=jnp.bfloat16):
    drawn = deviation * jax.random.normal(rng, shape, jnp.float32)
    if shards:
        drawn = drawn * steps_of(rng, shape, shards, -0.22, 0.18)
    return jnp.clip(drawn, -most, most).astype(kind)


def setup_inputs(seed: int = 0) -> dict:
    key_list = jax.random.split(jax.random.key(seed), 6)
    return {
        "activations": centred(key_list[0], (LAYERS, EXAMPLES, LEN, D), 1.0, 6.0, ((0, 16), (1, 2))),
        "out_grads": centred(key_list[1], (LAYERS, EXAMPLES, LEN, D), 1.0, 6.0, ((0, 16), (1, 2))),
        "proj_in": centred(key_list[2], (LAYERS, PROJ, D, K_IN), D ** -0.5, 0.09375, ((0, 16),)),
        "proj_out": centred(key_list[3], (LAYERS, PROJ, K_OUT, D), D ** -0.5, 0.09375, ((0, 16),)),
        "earlier_gram": draw_earlier_gram(jax.random.fold_in(key_list[5], 71), 0),
    }


def reference(activations, out_grads, proj_in, proj_out, earlier_gram):

    def layer_step(total, inputs):
        layer_act, layer_grad, layer_in, layer_out = inputs
        low_in = jnp.einsum('eld,pdm->pelm', layer_act.astype(jnp.float32), layer_in.astype(jnp.float32)).astype(jnp.bfloat16)
        low_out = jnp.einsum('pkd,eld->pekl', layer_out.astype(jnp.float32), layer_grad.astype(jnp.float32)).astype(jnp.bfloat16)
        partial_terms = jnp.einsum('pekl,pelm->ekm', low_out.astype(jnp.float32), low_in.astype(jnp.float32))
        return (total + partial_terms.reshape(partial_terms.shape[0], -1), None)
    start = jnp.zeros((EXAMPLES, K_OUT * K_IN), jnp.float32)
    summed, unused = lax.scan(layer_step, start, (activations, out_grads, proj_in, proj_out))
    features = summed / math.sqrt(LEN * LAYERS * PROJ)
    outer = jnp.dot(features.T, features, precision=lax.Precision.HIGHEST)
    return earlier_gram + outer / EXAMPLES
```

```python
import functools
import math

import jax
import jax.numpy as jnp
from jax import lax
from jax.experimental import pallas as pl
from jax.experimental.pallas import tpu as pltpu
from jax.sharding import PartitionSpec as P

MESH = pl.DeviceIdType.MESH
LANES = 128
SPLITS = 1
DEPTHS = (8,)
FIRST = 8


def split(x):
    hi = x.astype(jnp.bfloat16)
    lo = (x - hi.astype(jnp.float32)).astype(jnp.bfloat16)
    return hi, lo


def feature_kernel(
    n, groups, count, scale,
    act, grad, p_in, p_out, earlier,
    left, right, held,
    act_v, grad_v, in_v, out_v,
    phi, arrived, pieces, own, cols, row,
    load_sem, pair_sem, send_sem, recv_sem,
    col_send, col_recv, fwd_send, row_send, row_recv, held_sem,
):
    s = lax.axis_index("section")
    d = lax.axis_index("dp")
    chips = n // 2
    core = s % 2
    chip = s // 2
    partner = s + 1 - 2 * core

    draws, width, k_in = p_in.shape
    k_out = p_out.shape[1]
    tokens = act.shape[0]
    length = tokens // count

    copies = {}

    def fetch(key, src, dst):
        copies[key] = pltpu.make_async_copy(src, dst, load_sem.at[len(copies)])

    bounds = [count * i // SPLITS for i in range(SPLITS + 1)]
    for h in range(SPLITS):
        rs = pl.ds(bounds[h] * length, (bounds[h + 1] - bounds[h]) * length)
        pieces_of = DEPTHS[h]
        depth = width // pieces_of
        for c in range(pieces_of):
            cs = pl.ds(c * depth, depth)
            if h == 0:
                fetch(("p_in", c), p_in.at[:, cs], in_v.at[:, cs])
                fetch(("p_out", c), p_out.at[:, :, cs], out_v.at[:, :, cs])
            fetch(("act", h, c), act.at[rs, cs], act_v.at[rs, cs])
            fetch(("grad", h, c), grad.at[rs, cs], grad_v.at[rs, cs])
    queue = list(copies.values())
    for copy in queue[:FIRST]:
        copy.start()
    barrier = pltpu.get_barrier_semaphore()
    for g in range(groups):
        for i in range(n):
            pl.semaphore_signal(barrier, inc=1, device_id={"section": i, "dp": g}, device_id_type=MESH)
    for copy in queue[FIRST:]:
        copy.start()

    k_half = k_out // 2
    for h in range(SPLITS):
        lo, hi = bounds[h], bounds[h + 1]
        rs = slice(lo * length, hi * length)
        depth = width // DEPTHS[h]
        total_in = total_out = None
        for c in range(DEPTHS[h]):
            cs = slice(c * depth, (c + 1) * depth)
            if h == 0:
                copies["p_in", c].wait()
                copies["p_out", c].wait()
            copies["act", h, c].wait()
            copies["grad", h, c].wait()
            weights = jnp.concatenate([in_v[p, cs, :] for p in range(draws)], axis=1)
            term_in = jnp.dot(act_v[rs, cs], weights, preferred_element_type=jnp.float32)
            weights = out_v[:, :, cs].reshape(draws * k_out, depth)
            term_out = lax.dot_general(
                grad_v[rs, cs], weights, (((1,), (1,)), ((), ())), preferred_element_type=jnp.float32
            )
            total_in = term_in if total_in is None else total_in + term_in
            total_out = term_out if total_out is None else total_out + term_out
        if h == SPLITS - 1:
            hold = pltpu.make_async_copy(earlier, held, held_sem)
            hold.start()
        in_part = total_in.astype(jnp.bfloat16)
        for e in range(lo, hi):
            ts = slice((e - lo) * length, (e - lo + 1) * length)
            lhs = jnp.concatenate([total_out[ts, p * k_out:(p + 1) * k_out] for p in range(draws)], axis=0)
            rhs = jnp.concatenate([in_part[ts, p * k_in:(p + 1) * k_in] for p in range(draws)], axis=0)
            phi[pl.ds(e, k_out, stride=count), :] = jnp.dot(
                lhs.T.astype(jnp.bfloat16), rhs, preferred_element_type=jnp.float32
            )

    def remote(src, dst, ssem, rsem, section, dp):
        return pltpu.make_async_remote_copy(
            src_ref=src, dst_ref=dst, send_sem=ssem, recv_sem=rsem,
            device_id={"section": section, "dp": dp}, device_id_type=MESH,
        )

    half_rows = k_half * count
    pl.semaphore_wait(barrier, n * groups)
    theirs = phi.at[pl.ds(pl.multiple_of((1 - core) * half_rows, half_rows), half_rows)]
    mine = phi.at[pl.ds(pl.multiple_of(core * half_rows, half_rows), half_rows)]
    swap = remote(theirs, arrived, pair_sem.at[0], pair_sem.at[1], partner, d)
    swap.start()
    swap.wait_recv()

    def across(c, i):
        bit = 1
        while bit < chips:
            if i & bit:
                c = c + bit * (1 - 2 * ((c // bit) % 2))
            bit *= 2
        return c

    k_chunk = k_half // chips
    rows = k_chunk * count
    sends = []
    for i in range(chips - 1, 0, -1):
        to = across(chip, i)
        ks = pl.ds(pl.multiple_of(to * rows, rows), rows)
        mine[ks, :] = mine[ks, :] + arrived[ks, :]
        copy = remote(mine.at[ks], pieces.at[i - 1], send_sem.at[i - 1], recv_sem.at[i - 1], 2 * to + core, d)
        copy.start()
        sends.append(copy)
    ks = pl.ds(pl.multiple_of(chip * rows, rows), rows)
    total = mine[ks, :] + arrived[ks, :]
    for i in range(1, chips):
        sends[chips - 1 - i].wait_recv()
        total = total + pieces[i - 1]

    own[...] = total

    per_group = n // groups
    q = core * chips + chip
    own_slot = q % per_group
    home = q // per_group
    at_home = home == d

    def col_copy(i):
        return remote(
            own, cols.at[own_slot, d], col_send.at[i], col_recv.at[own_slot, d], 2 * across(chip, i) + core, home
        )

    def pair_copy():
        return remote(own, cols.at[own_slot, d], col_send.at[0], col_recv.at[own_slot, d], partner, d)

    def row_copy(g):
        return remote(own, row.at[d], row_send.at[g], row_recv.at[d], q, g)

    for i in range(chips - 1, 0, -1):
        col_copy(i).start()

    @pl.when(at_home)
    def _():
        pair_copy().start()
        cols[own_slot, d] = own[...]

    @pl.when(jnp.logical_not(at_home))
    def _():
        col_copy(0).start()

    for g in range(groups):
        needed = home != g
        here = jnp.logical_and(q == s, d == g)

        @pl.when(jnp.logical_and(needed, jnp.logical_not(here)))
        def _():
            row_copy(g).start()

        @pl.when(jnp.logical_and(needed, here))
        def _():
            row[d] = own[...]

    def forward(j, g):
        return remote(cols.at[j, g], cols.at[j, g], fwd_send.at[j, g], col_recv.at[j, g], partner, d)

    for i in range(per_group):
        j = across(chip, i) % per_group
        owner = d * per_group + j
        for g in range(groups):
            other = jnp.logical_or(owner != q, d != g)

            @pl.when(other)
            def _():
                forward(j, g).wait_recv()

            @pl.when(jnp.logical_and(other, owner // chips == core))
            def _():
                forward(j, g).start()

        for k in range(k_chunk):
            hi, lo = split(jnp.concatenate([cols[j, g, k * count:(k + 1) * count] for g in range(groups)], axis=0))
            at = pl.multiple_of((j * k_chunk + k) * LANES, LANES)
            right[:, pl.ds(at, LANES)] = jnp.concatenate([hi, hi, lo], axis=0)

    for g in range(groups):

        @pl.when(jnp.logical_and(s // per_group != d, jnp.logical_or(q != s, d != g)))
        def _():
            remote(own, row.at[g], row_send.at[g], row_recv.at[g], q, d).wait_recv()

    @pl.when(s // per_group == d)
    def _():
        row[...] = cols[s % per_group]

    for k in range(k_chunk):
        hi, lo = split(jnp.concatenate([row[g, k * count:(k + 1) * count] for g in range(groups)], axis=0) * scale)
        left[:, k * LANES:(k + 1) * LANES] = jnp.concatenate([hi, lo, hi], axis=0)

    hold.wait()
    swap.wait_send()
    for copy in sends:
        copy.wait_send()

    for i in range(1, chips):
        col_copy(i).wait_send()

    @pl.when(at_home)
    def _():
        pair_copy().wait_send()

    @pl.when(jnp.logical_not(at_home))
    def _():
        col_copy(0).wait_send()

    for g in range(groups):

        @pl.when(jnp.logical_and(home != g, jnp.logical_or(q != s, d != g)))
        def _():
            row_copy(g).wait_send()

    for j in range(per_group):
        owner = d * per_group + j
        for g in range(groups):

            @pl.when(jnp.logical_and(jnp.logical_or(owner != q, d != g), owner // chips == core))
            def _():
                forward(j, g).wait_send()


def gram_kernel(tiles, left, right, earlier, out, tile_v, sem):
    columns = right.shape[1] // tiles
    lhs = left[...].T
    copies = []
    for i in range(tiles):
        cs = slice(i * columns, (i + 1) * columns)
        tile_v[:, cs] = earlier[:, cs] + jnp.dot(lhs, right[:, cs], preferred_element_type=jnp.float32)
        copy = pltpu.make_async_copy(
            tile_v.at[:, pl.ds(i * columns, columns)], out.at[:, pl.ds(i * columns, columns)], sem.at[i]
        )
        copy.start()
        copies.append(copy)
    for copy in copies:
        copy.wait()


def per_device(activations, out_grads, proj_in, proj_out, earlier_gram):
    n = lax.axis_size("section")
    groups = lax.axis_size("dp")
    _, count, length, width = activations.shape
    _, draws, _, k_in = proj_in.shape
    k_out = proj_out.shape[2]
    tokens = count * length
    examples = count * groups
    scale = 1.0 / (length * n * draws) / examples
    row_width, col_width = earlier_gram.shape
    chips = n // 2
    k_half = k_out // 2
    k_chunk = k_half // chips
    per_group = n // groups
    any_spec = pl.BlockSpec(memory_space=pl.ANY)
    vmem_spec = pl.BlockSpec(memory_space=pltpu.VMEM)
    f32, bf16 = jnp.float32, jnp.bfloat16
    dma = pltpu.SemaphoreType.DMA

    left, right, held = pl.pallas_call(
        functools.partial(feature_kernel, n, groups, count, scale),
        out_shape=(
            pltpu.VMEM((3 * examples, row_width), bf16),
            pltpu.VMEM((3 * examples, col_width), bf16),
            pltpu.VMEM((row_width, col_width), f32),
        ),
        in_specs=[any_spec] * 5,
        out_specs=(vmem_spec, vmem_spec, vmem_spec),
        scratch_shapes=[
            pltpu.VMEM((tokens, width), bf16),
            pltpu.VMEM((tokens, width), bf16),
            pltpu.VMEM((draws, width, k_in), bf16),
            pltpu.VMEM((draws, k_out, width), bf16),
            pltpu.VMEM((k_out * count, k_in), f32),
            pltpu.VMEM((k_half * count, k_in), f32),
            pltpu.VMEM((chips - 1, k_chunk * count, k_in), f32),
            pltpu.VMEM((k_chunk * count, k_in), f32),
            pltpu.VMEM((per_group, groups, k_chunk * count, k_in), f32),
            pltpu.VMEM((groups, k_chunk * count, k_in), f32),
            dma((2 * (DEPTHS[0] + sum(DEPTHS)),)),
            dma((2,)),
            dma((chips - 1,)),
            dma((chips - 1,)),
            dma((chips,)),
            dma((per_group, groups)),
            dma((per_group, groups)),
            dma((groups,)),
            dma((groups,)),
            dma,
        ],
        compiler_params=pltpu.CompilerParams(
            collective_id=0, has_side_effects=True, vmem_limit_bytes=52 << 20
        ),
        name="features",
    )(
        activations.reshape(tokens, width),
        out_grads.reshape(tokens, width),
        proj_in[0],
        proj_out[0],
        earlier_gram,
    )
    tiles = 8
    return pl.pallas_call(
        functools.partial(gram_kernel, tiles),
        out_shape=jax.ShapeDtypeStruct((row_width, col_width), f32),
        in_specs=[vmem_spec, vmem_spec, vmem_spec],
        out_specs=any_spec,
        scratch_shapes=[pltpu.VMEM((row_width, col_width), f32), dma((tiles,))],
        compiler_params=pltpu.CompilerParams(vmem_limit_bytes=28 << 20),
        name="gram",
    )(left, right, held)


def solution(mesh):
    return jax.shard_map(
        per_device,
        mesh=mesh,
        in_specs=(
            P("section", "dp", None, None),
            P("section", "dp", None, None),
            P("section", None, None, None),
            P("section", None, None, None),
            P("section", "dp"),
        ),
        out_specs=P("section", "dp"),
        check_vma=False,
    )
```

```python
import functools
import math

import jax
import jax.numpy as jnp
from jax import lax
from jax.experimental import pallas as pl
from jax.experimental.pallas import tpu as pltpu
from jax.sharding import PartitionSpec as P

MESH = pl.DeviceIdType.MESH
LANES = 128
PIECES = 8
FIRST = 2


def split(x):
    hi = x.astype(jnp.bfloat16)
    lo = (x - hi.astype(jnp.float32)).astype(jnp.bfloat16)
    return hi, lo


def feature_kernel(
    n, groups, count, scale,
    act, grad, p_in, p_out, earlier,
    left, right, held,
    act_v, grad_v, in_v, out_v,
    phi, arrived, pieces, own, cols, row,
    load_sem, pair_sem, send_sem, recv_sem, col_recv, row_send, row_recv, held_sem,
):
    s = lax.axis_index("section")
    d = lax.axis_index("dp")
    chips = n // 2
    core = s % 2
    chip = s // 2
    partner = s + 1 - 2 * core

    draws, width, k_in = p_in.shape
    k_out = p_out.shape[1]
    tokens = act.shape[0]
    length = tokens // count

    depth = width // PIECES
    loads = []
    for c in range(PIECES):
        cs = pl.ds(c * depth, depth)
        sem = load_sem.at[c]
        loads.append([
            pltpu.make_async_copy(p_in.at[:, cs], in_v.at[:, cs], sem),
            pltpu.make_async_copy(p_out.at[:, :, cs], out_v.at[:, :, cs], sem),
            pltpu.make_async_copy(act.at[:, cs], act_v.at[:, cs], sem),
            pltpu.make_async_copy(grad.at[:, cs], grad_v.at[:, cs], sem),
        ])

    def start(some):
        for piece in some:
            for copy in piece:
                copy.start()

    start(loads[:FIRST])
    barrier = pltpu.get_barrier_semaphore()
    for g in range(groups):
        for i in range(n):
            pl.semaphore_signal(barrier, inc=1, device_id={"section": i, "dp": g}, device_id_type=MESH)
    start(loads[FIRST:])

    piece_rows = depth * (draws * (k_in + k_out) + 2 * tokens) // width
    total_in = total_out = None
    for c in range(PIECES):
        cs = slice(c * depth, (c + 1) * depth)
        pltpu.make_async_copy(act.at[pl.ds(0, piece_rows)], act_v.at[pl.ds(0, piece_rows)], load_sem.at[c]).wait()
        weights = jnp.concatenate([in_v[p, cs, :] for p in range(draws)], axis=1)
        term_in = jnp.dot(act_v[:, cs], weights, preferred_element_type=jnp.float32)
        weights = out_v[:, :, cs].reshape(draws * k_out, depth)
        term_out = lax.dot_general(
            grad_v[:, cs], weights, (((1,), (1,)), ((), ())), preferred_element_type=jnp.float32
        )
        total_in = term_in if total_in is None else total_in + term_in
        total_out = term_out if total_out is None else total_out + term_out
    low_in = total_in.astype(jnp.bfloat16)
    k_half = k_out // 2
    half_rows = k_half * count
    for e in range(count):
        ts = slice(e * length, (e + 1) * length)
        lhs = jnp.concatenate([total_out[ts, p * k_out:(p + 1) * k_out] for p in range(draws)], axis=0)
        rhs = jnp.concatenate([low_in[ts, p * k_in:(p + 1) * k_in] for p in range(draws)], axis=0)
        phi[pl.ds(e, k_out, stride=count), :] = jnp.dot(
            lhs.T.astype(jnp.bfloat16), rhs, preferred_element_type=jnp.float32
        )
    def remote(src, dst, ssem, rsem, section, dp):
        return pltpu.make_async_remote_copy(
            src_ref=src, dst_ref=dst, send_sem=ssem, recv_sem=rsem,
            device_id={"section": section, "dp": dp}, device_id_type=MESH,
        )

    pl.semaphore_wait(barrier, n * groups)
    theirs = phi.at[pl.ds(pl.multiple_of((1 - core) * half_rows, half_rows), half_rows)]
    mine = phi.at[pl.ds(pl.multiple_of(core * half_rows, half_rows), half_rows)]
    swap = remote(theirs, arrived, pair_sem.at[0], pair_sem.at[1], partner, d)
    swap.start()
    swap.wait_recv()

    def across(c, i):
        bit = 1
        while bit < chips:
            if i & bit:
                c = c + bit * (1 - 2 * ((c // bit) % 2))
            bit *= 2
        return c

    k_chunk = k_half // chips
    rows = k_chunk * count
    for i in range(chips - 1, 0, -1):
        to = across(chip, i)
        ks = pl.ds(pl.multiple_of(to * rows, rows), rows)
        mine[ks, :] = mine[ks, :] + arrived[ks, :]
        remote(mine.at[ks], pieces.at[i - 1], send_sem.at[0], recv_sem.at[0], 2 * to + core, d).start()
    hold = pltpu.make_async_copy(earlier, held, held_sem)
    hold.start()
    ks = pl.ds(pl.multiple_of(chip * rows, rows), rows)
    total = mine[ks, :] + arrived[ks, :]
    exchange = remote(pieces, pieces, send_sem.at[0], recv_sem.at[0], partner, d)
    exchange.wait_recv()
    for i in range(1, chips):
        total = total + pieces[i - 1]
    own[...] = total

    per_group = n // groups
    q = core * chips + chip
    own_slot = q % per_group
    home = q // per_group
    at_home = home == d

    def col_copy(to):
        return remote(own, cols.at[own_slot, d], send_sem.at[1], col_recv.at[own_slot], 2 * to + core, home)

    for i in range(chips - 1):
        col_copy(jnp.where(chip <= i, i + 1, i)).start()
    cross = jnp.logical_not(at_home)

    @pl.when(at_home)
    def _():
        remote(own, cols.at[own_slot, d], send_sem.at[1], col_recv.at[own_slot], partner, d).start()
        cols[own_slot, d] = own[...]

    @pl.when(cross)
    def _():
        col_copy(chip).start()

    row_here = jnp.logical_and(q == s, home != d)
    for g in range(groups):
        here = jnp.logical_and(q == s, d == g)

        @pl.when(jnp.logical_and(home != g, jnp.logical_not(here)))
        def _():
            remote(own, row.at[d], row_send.at[g], row_recv.at[d], q, g).start()

        @pl.when(jnp.logical_and(home != g, here))
        def _():
            row[d] = own[...]

    def forward(j, lo, size, sem):
        ref = cols.at[j, pl.ds(lo, size)]
        return remote(ref, ref, send_sem.at[sem], col_recv.at[j], partner, d)

    passes = d * per_group // chips == core
    for i in range(per_group):
        j = across(chip, i) % per_group
        mixed = d * per_group + j == q

        @pl.when(jnp.logical_not(mixed))
        def _():
            forward(j, 0, groups, 2).wait_recv()

            @pl.when(passes)
            def _():
                forward(j, 0, groups, 2).start()

        @pl.when(mixed)
        def _():
            forward(j, 0, groups - 1, 3).wait_recv()
            for g in range(groups):

                @pl.when(d != g)
                def _():
                    forward(j, g, 1, 3).start()

        for k in range(k_chunk):
            hi, lo = split(jnp.concatenate([cols[j, g, k * count:(k + 1) * count] for g in range(groups)], axis=0))
            at = pl.multiple_of((j * k_chunk + k) * LANES, LANES)
            right[:, pl.ds(at, LANES)] = jnp.concatenate([hi, hi, lo], axis=0)

    for g in range(groups):

        @pl.when(jnp.logical_and(s // per_group != d, jnp.logical_or(q != s, d != g)))
        def _():
            remote(own, row.at[g], row_send.at[g], row_recv.at[g], q, d).wait_recv()

    @pl.when(s // per_group == d)
    def _():
        row[...] = cols[s % per_group]

    for k in range(k_chunk):
        hi, lo = split(jnp.concatenate([row[g, k * count:(k + 1) * count] for g in range(groups)], axis=0) * scale)
        left[:, k * LANES:(k + 1) * LANES] = jnp.concatenate([hi, lo, hi], axis=0)

    hold.wait()
    swap.wait_send()
    exchange.wait_send()
    remote(arrived, arrived, send_sem.at[1], recv_sem.at[0], partner, d).wait_send()
    for g in range(groups):

        @pl.when(jnp.logical_and(home != g, jnp.logical_or(q != s, d != g)))
        def _():
            remote(own, row.at[d], row_send.at[g], row_recv.at[d], q, g).wait_send()

    def forwarded(count, sem):
        ref = cols.at[pl.ds(0, count)]
        remote(ref, ref, send_sem.at[sem], recv_sem.at[0], partner, d).wait_send()

    @pl.when(at_home)
    def _():
        forwarded(per_group - 1, 2)
        forward(0, 0, groups - 1, 3).wait_send()

    @pl.when(jnp.logical_and(passes, cross))
    def _():
        forwarded(per_group, 2)


def gram_kernel(tiles, left, right, earlier, out, tile_v, sem):
    columns = right.shape[1] // tiles
    lhs = left[...].T
    copies = []
    for i in range(tiles):
        cs = slice(i * columns, (i + 1) * columns)
        tile_v[:, cs] = earlier[:, cs] + jnp.dot(lhs, right[:, cs], preferred_element_type=jnp.float32)
        copy = pltpu.make_async_copy(
            tile_v.at[:, pl.ds(i * columns, columns)], out.at[:, pl.ds(i * columns, columns)], sem.at[i]
        )
        copy.start()
        copies.append(copy)
    for copy in copies:
        copy.wait()


def per_device(activations, out_grads, proj_in, proj_out, earlier_gram):
    n = lax.axis_size("section")
    groups = lax.axis_size("dp")
    _, count, length, width = activations.shape
    _, draws, _, k_in = proj_in.shape
    k_out = proj_out.shape[2]
    tokens = count * length
    examples = count * groups
    scale = 1.0 / (length * n * draws) / examples
    row_width, col_width = earlier_gram.shape
    chips = n // 2
    k_half = k_out // 2
    k_chunk = k_half // chips
    per_group = n // groups
    any_spec = pl.BlockSpec(memory_space=pl.ANY)
    vmem_spec = pl.BlockSpec(memory_space=pltpu.VMEM)
    f32, bf16 = jnp.float32, jnp.bfloat16
    dma = pltpu.SemaphoreType.DMA

    left, right, held = pl.pallas_call(
        functools.partial(feature_kernel, n, groups, count, scale),
        out_shape=(
            pltpu.VMEM((3 * examples, row_width), bf16),
            pltpu.VMEM((3 * examples, col_width), bf16),
            pltpu.VMEM((row_width, col_width), f32),
        ),
        in_specs=[any_spec] * 5,
        out_specs=(vmem_spec, vmem_spec, vmem_spec),
        scratch_shapes=[
            pltpu.VMEM((tokens, width), bf16),
            pltpu.VMEM((tokens, width), bf16),
            pltpu.VMEM((draws, width, k_in), bf16),
            pltpu.VMEM((draws, k_out, width), bf16),
            pltpu.VMEM((k_out * count, k_in), f32),
            pltpu.VMEM((k_half * count, k_in), f32),
            pltpu.VMEM((chips - 1, k_chunk * count, k_in), f32),
            pltpu.VMEM((k_chunk * count, k_in), f32),
            pltpu.VMEM((per_group, groups, k_chunk * count, k_in), f32),
            pltpu.VMEM((groups, k_chunk * count, k_in), f32),
            dma((PIECES,)),
            dma((2,)),
            dma((4,)),
            dma((1,)),
            dma((per_group,)),
            dma((groups,)),
            dma((groups,)),
            dma,
        ],
        compiler_params=pltpu.CompilerParams(
            collective_id=0, has_side_effects=True, vmem_limit_bytes=52 << 20
        ),
        name="features",
    )(
        activations.reshape(tokens, width),
        out_grads.reshape(tokens, width),
        proj_in[0],
        proj_out[0],
        earlier_gram,
    )
    tiles = 8
    return pl.pallas_call(
        functools.partial(gram_kernel, tiles),
        out_shape=jax.ShapeDtypeStruct((row_width, col_width), f32),
        in_specs=[vmem_spec, vmem_spec, vmem_spec],
        out_specs=any_spec,
        scratch_shapes=[pltpu.VMEM((row_width, col_width), f32), dma((tiles,))],
        compiler_params=pltpu.CompilerParams(vmem_limit_bytes=28 << 20),
        name="gram",
    )(left, right, held)


def solution(mesh):
    return jax.shard_map(
        per_device,
        mesh=mesh,
        in_specs=(
            P("section", "dp", None, None),
            P("section", "dp", None, None),
            P("section", None, None, None),
            P("section", None, None, None),
            P("section", "dp"),
        ),
        out_specs=P("section", "dp"),
        check_vma=False,
    )
```

```python
import functools
import math

import jax
import jax.numpy as jnp
from jax import lax
from jax.experimental import pallas as pl
from jax.experimental.pallas import tpu as pltpu
from jax.sharding import PartitionSpec as P

MESH = pl.DeviceIdType.MESH
LANES = 128
PIECES = (3, 3, 3, 3, 2, 1, 1)
FIRST = 2


def split(x):
    hi = x.astype(jnp.bfloat16)
    lo = (x - hi.astype(jnp.float32)).astype(jnp.bfloat16)
    return hi, lo


def feature_kernel(
    n, groups, count, scale,
    act, grad, p_in, p_out, earlier,
    left, right, held,
    act_v, grad_v, in_v, out_v,
    phi, arrived, pieces, own, cols, row,
    load_sem, pair_sem, send_sem, recv_sem, col_recv, row_send, row_recv, held_sem,
):
    s = lax.axis_index("section")
    d = lax.axis_index("dp")
    chips = n // 2
    core = s % 2
    chip = s // 2
    partner = s + 1 - 2 * core

    draws, width, k_in = p_in.shape
    k_out = p_out.shape[1]
    tokens = act.shape[0]
    length = tokens // count

    loads, spans, row_counts = [], [], []
    at = 0
    for c, part in enumerate(PIECES):
        depth = width * part // sum(PIECES)
        spans.append(slice(at, at + depth))
        row_counts.append(depth * (draws * (k_in + k_out) + 2 * tokens) // width)
        cs = pl.ds(at, depth)
        at += depth
        sem = load_sem.at[c]
        loads.append([
            pltpu.make_async_copy(p_in.at[:, cs], in_v.at[:, cs], sem),
            pltpu.make_async_copy(p_out.at[:, :, cs], out_v.at[:, :, cs], sem),
            pltpu.make_async_copy(act.at[:, cs], act_v.at[:, cs], sem),
            pltpu.make_async_copy(grad.at[:, cs], grad_v.at[:, cs], sem),
        ])

    def start(some):
        for piece in some:
            for copy in piece:
                copy.start()

    start(loads[:FIRST])
    barrier = pltpu.get_barrier_semaphore()
    for g in range(groups):
        for i in range(n):
            pl.semaphore_signal(barrier, inc=1, device_id={"section": i, "dp": g}, device_id_type=MESH)
    start(loads[FIRST:])

    total_in = total_out = None
    for c, (cs, piece_rows) in enumerate(zip(spans, row_counts)):
        pltpu.make_async_copy(act.at[pl.ds(0, piece_rows)], act_v.at[pl.ds(0, piece_rows)], load_sem.at[c]).wait()
        weights = jnp.concatenate([in_v[p, cs, :] for p in range(draws)], axis=1)
        term_in = jnp.dot(act_v[:, cs], weights, preferred_element_type=jnp.float32)
        weights = out_v[:, :, cs].reshape(draws * k_out, cs.stop - cs.start)
        term_out = lax.dot_general(
            grad_v[:, cs], weights, (((1,), (1,)), ((), ())), preferred_element_type=jnp.float32
        )
        total_in = term_in if total_in is None else total_in + term_in
        total_out = term_out if total_out is None else total_out + term_out
    low_in = total_in.astype(jnp.bfloat16)
    k_half = k_out // 2
    half_rows = k_half * count
    for e in range(count):
        ts = slice(e * length, (e + 1) * length)
        lhs = jnp.concatenate([total_out[ts, p * k_out:(p + 1) * k_out] for p in range(draws)], axis=0)
        rhs = jnp.concatenate([low_in[ts, p * k_in:(p + 1) * k_in] for p in range(draws)], axis=0)
        phi[pl.ds(e, k_out, stride=count), :] = jnp.dot(
            lhs.T.astype(jnp.bfloat16), rhs, preferred_element_type=jnp.float32
        )
    def remote(src, dst, ssem, rsem, section, dp):
        return pltpu.make_async_remote_copy(
            src_ref=src, dst_ref=dst, send_sem=ssem, recv_sem=rsem,
            device_id={"section": section, "dp": dp}, device_id_type=MESH,
        )

    pl.semaphore_wait(barrier, n * groups)
    theirs = phi.at[pl.ds(pl.multiple_of((1 - core) * half_rows, half_rows), half_rows)]
    mine = phi.at[pl.ds(pl.multiple_of(core * half_rows, half_rows), half_rows)]
    swap = remote(theirs, arrived, pair_sem.at[0], pair_sem.at[1], partner, d)
    swap.start()
    swap.wait_recv()

    def across(c, i):
        bit = 1
        while bit < chips:
            if i & bit:
                c = c + bit * (1 - 2 * ((c // bit) % 2))
            bit *= 2
        return c

    k_chunk = k_half // chips
    rows = k_chunk * count
    turns = [2 * (m ^ m // 2) + b for m in range(1, chips // 2) for b in (0, 1)] + [1]
    for i in turns:
        to = across(chip, i)
        ks = pl.ds(pl.multiple_of(to * rows, rows), rows)
        mine[ks, :] = mine[ks, :] + arrived[ks, :]
        remote(mine.at[ks], pieces.at[i - 1], send_sem.at[0], recv_sem.at[0], 2 * to + core, d).start()
    hold = pltpu.make_async_copy(earlier, held, held_sem)
    hold.start()
    ks = pl.ds(pl.multiple_of(chip * rows, rows), rows)
    total = mine[ks, :] + arrived[ks, :]
    exchange = remote(pieces, pieces, send_sem.at[0], recv_sem.at[0], partner, d)
    exchange.wait_recv()
    for i in range(1, chips):
        total = total + pieces[i - 1]
    own[...] = total

    per_group = n // groups
    q = core * chips + chip
    own_slot = q % per_group
    home = q // per_group
    at_home = home == d

    def col_copy(to):
        return remote(own, cols.at[own_slot, d], send_sem.at[1], col_recv.at[own_slot], 2 * to + core, home)

    for i in range(chips - 1):
        col_copy(jnp.where(chip <= i, i + 1, i)).start()
    cross = jnp.logical_not(at_home)

    @pl.when(at_home)
    def _():
        remote(own, cols.at[own_slot, d], send_sem.at[1], col_recv.at[own_slot], partner, d).start()
        cols[own_slot, d] = own[...]

    @pl.when(cross)
    def _():
        col_copy(chip).start()

    row_here = jnp.logical_and(q == s, home != d)
    for g in range(groups):
        here = jnp.logical_and(q == s, d == g)

        @pl.when(jnp.logical_and(home != g, jnp.logical_not(here)))
        def _():
            remote(own, row.at[d], row_send.at[g], row_recv.at[d], q, g).start()

        @pl.when(jnp.logical_and(home != g, here))
        def _():
            row[d] = own[...]

    def forward(j, lo, size, sem):
        ref = cols.at[j, pl.ds(lo, size)]
        return remote(ref, ref, send_sem.at[sem], col_recv.at[j], partner, d)

    passes = d * per_group // chips == core
    for i in range(per_group):
        j = across(chip, i) % per_group
        mixed = d * per_group + j == q

        @pl.when(jnp.logical_not(mixed))
        def _():
            forward(j, 0, groups, 2).wait_recv()

            @pl.when(passes)
            def _():
                forward(j, 0, groups, 2).start()

        @pl.when(mixed)
        def _():
            forward(j, 0, groups - 1, 3).wait_recv()
            for g in range(groups):

                @pl.when(d != g)
                def _():
                    forward(j, g, 1, 3).start()

        for k in range(k_chunk):
            hi, lo = split(jnp.concatenate([cols[j, g, k * count:(k + 1) * count] for g in range(groups)], axis=0))
            at = pl.multiple_of((j * k_chunk + k) * LANES, LANES)
            right[:, pl.ds(at, LANES)] = jnp.concatenate([hi, hi, lo], axis=0)

    for g in range(groups):

        @pl.when(jnp.logical_and(s // per_group != d, jnp.logical_or(q != s, d != g)))
        def _():
            remote(own, row.at[g], row_send.at[g], row_recv.at[g], q, d).wait_recv()

    @pl.when(s // per_group == d)
    def _():
        row[...] = cols[s % per_group]

    for k in range(k_chunk):
        hi, lo = split(jnp.concatenate([row[g, k * count:(k + 1) * count] for g in range(groups)], axis=0) * scale)
        left[:, k * LANES:(k + 1) * LANES] = jnp.concatenate([hi, lo, hi], axis=0)

    hold.wait()
    swap.wait_send()
    exchange.wait_send()
    remote(arrived, arrived, send_sem.at[1], recv_sem.at[0], partner, d).wait_send()
    for g in range(groups):

        @pl.when(jnp.logical_and(home != g, jnp.logical_or(q != s, d != g)))
        def _():
            remote(own, row.at[d], row_send.at[g], row_recv.at[d], q, g).wait_send()

    def forwarded(count, sem):
        ref = cols.at[pl.ds(0, count)]
        remote(ref, ref, send_sem.at[sem], recv_sem.at[0], partner, d).wait_send()

    @pl.when(at_home)
    def _():
        forwarded(per_group - 1, 2)
        forward(0, 0, groups - 1, 3).wait_send()

    @pl.when(jnp.logical_and(passes, cross))
    def _():
        forwarded(per_group, 2)


def gram_kernel(tiles, left, right, earlier, out, tile_v, sem):
    height = earlier.shape[0] // tiles
    lhs = left[...].T
    copies = []
    for i in range(tiles):
        rs = slice(i * height, (i + 1) * height)
        tile_v[rs, :] = earlier[rs, :] + jnp.dot(lhs[rs], right[...], preferred_element_type=jnp.float32)
        copy = pltpu.make_async_copy(
            tile_v.at[pl.ds(i * height, height)], out.at[pl.ds(i * height, height)], sem.at[0]
        )
        copy.start()
        copies.append(copy)
    pltpu.make_async_copy(tile_v, out, sem.at[0]).wait()


def per_device(activations, out_grads, proj_in, proj_out, earlier_gram):
    n = lax.axis_size("section")
    groups = lax.axis_size("dp")
    _, count, length, width = activations.shape
    _, draws, _, k_in = proj_in.shape
    k_out = proj_out.shape[2]
    tokens = count * length
    examples = count * groups
    scale = 1.0 / (length * n * draws) / examples
    row_width, col_width = earlier_gram.shape
    chips = n // 2
    k_half = k_out // 2
    k_chunk = k_half // chips
    per_group = n // groups
    any_spec = pl.BlockSpec(memory_space=pl.ANY)
    vmem_spec = pl.BlockSpec(memory_space=pltpu.VMEM)
    f32, bf16 = jnp.float32, jnp.bfloat16
    dma = pltpu.SemaphoreType.DMA

    left, right, held = pl.pallas_call(
        functools.partial(feature_kernel, n, groups, count, scale),
        out_shape=(
            pltpu.VMEM((3 * examples, row_width), bf16),
            pltpu.VMEM((3 * examples, col_width), bf16),
            pltpu.VMEM((row_width, col_width), f32),
        ),
        in_specs=[any_spec] * 5,
        out_specs=(vmem_spec, vmem_spec, vmem_spec),
        scratch_shapes=[
            pltpu.VMEM((tokens, width), bf16),
            pltpu.VMEM((tokens, width), bf16),
            pltpu.VMEM((draws, width, k_in), bf16),
            pltpu.VMEM((draws, k_out, width), bf16),
            pltpu.VMEM((k_out * count, k_in), f32),
            pltpu.VMEM((k_half * count, k_in), f32),
            pltpu.VMEM((chips - 1, k_chunk * count, k_in), f32),
            pltpu.VMEM((k_chunk * count, k_in), f32),
            pltpu.VMEM((per_group, groups, k_chunk * count, k_in), f32),
            pltpu.VMEM((groups, k_chunk * count, k_in), f32),
            dma((len(PIECES),)),
            dma((2,)),
            dma((4,)),
            dma((1,)),
            dma((per_group,)),
            dma((groups,)),
            dma((groups,)),
            dma,
        ],
        compiler_params=pltpu.CompilerParams(
            collective_id=0, has_side_effects=True, vmem_limit_bytes=52 << 20
        ),
        name="features",
    )(
        activations.reshape(tokens, width),
        out_grads.reshape(tokens, width),
        proj_in[0],
        proj_out[0],
        earlier_gram,
    )
    tiles = 16
    return pl.pallas_call(
        functools.partial(gram_kernel, tiles),
        out_shape=jax.ShapeDtypeStruct((row_width, col_width), f32),
        in_specs=[vmem_spec, vmem_spec, vmem_spec],
        out_specs=any_spec,
        scratch_shapes=[pltpu.VMEM((row_width, col_width), f32), dma((1,))],
        compiler_params=pltpu.CompilerParams(vmem_limit_bytes=28 << 20),
        name="gram",
    )(left, right, held)


def solution(mesh):
    return jax.shard_map(
        per_device,
        mesh=mesh,
        in_specs=(
            P("section", "dp", None, None),
            P("section", "dp", None, None),
            P("section", None, None, None),
            P("section", None, None, None),
            P("section", "dp"),
        ),
        out_specs=P("section", "dp"),
        check_vma=False,
    )
```

```python
import functools
import math

import jax
import jax.numpy as jnp
from jax import lax
from jax.experimental import pallas as pl
from jax.experimental.pallas import tpu as pltpu
from jax.sharding import PartitionSpec as P

MESH = pl.DeviceIdType.MESH
LANES = 128
PIECES = ((2, 2, 2, 2), (2, 2, 2, 2))
FIRST = 2
TURN = 1


def split(x):
    hi = x.astype(jnp.bfloat16)
    lo = (x - hi.astype(jnp.float32)).astype(jnp.bfloat16)
    return hi, lo


def feature_kernel(
    n, groups, count, scale,
    act, grad, p_in, p_out, earlier,
    left, right, held,
    act_v, grad_v, in_v, out_v,
    theirs, mine, arrived, pieces, own, cols, row,
    load_sem, pair_sem, send_sem, recv_sem, col_recv, row_send, row_recv, held_sem,
):
    s = lax.axis_index("section")
    d = lax.axis_index("dp")
    chips = n // 2
    core = s % 2
    chip = s // 2
    partner = s + 1 - 2 * core

    draws, width, k_in = p_in.shape
    k_out = p_out.shape[1]
    tokens = act.shape[0]
    length = tokens // count

    parts = len(PIECES)
    part_count = count // parts
    part_tokens = part_count * length
    k_half = k_out // 2
    half_rows = k_half * part_count

    loads, spans = [], []
    for p, shares in enumerate(PIECES):
        rs = slice(p * part_tokens, (p + 1) * part_tokens)
        spans.append([])
        at = 0
        for share in shares:
            depth = width * share // sum(shares)
            cs = slice(at, at + depth)
            at += depth
            sem = load_sem.at[len(loads)]
            copies = []
            if p == 0:
                copies.append(pltpu.make_async_copy(p_in.at[:, cs], in_v.at[:, cs], sem))
                copies.append(pltpu.make_async_copy(p_out.at[:, :, cs], out_v.at[:, :, cs], sem))
            copies.append(pltpu.make_async_copy(act.at[rs, cs], act_v.at[rs, cs], sem))
            copies.append(pltpu.make_async_copy(grad.at[rs, cs], grad_v.at[rs, cs], sem))
            taken = depth * (2 * part_tokens + (draws * (k_in + k_out) if p == 0 else 0)) // width
            whole = pltpu.make_async_copy(act.at[pl.ds(0, taken)], act_v.at[pl.ds(0, taken)], sem)
            spans[p].append((cs, whole))
            loads.append(copies)

    def start(some):
        for copies in some:
            for copy in copies:
                copy.start()

    start(loads[:FIRST])
    barrier = pltpu.get_barrier_semaphore()
    for g in range(groups):
        for i in range(n):
            pl.semaphore_signal(barrier, inc=1, device_id={"section": i, "dp": g}, device_id_type=MESH)
    start(loads[FIRST:])

    def project(p, pieces_now, sums):
        rs = slice(p * part_tokens, (p + 1) * part_tokens)
        for cs, whole in pieces_now:
            whole.wait()
            weights = jnp.concatenate([in_v[i, cs, :] for i in range(draws)], axis=1)
            term_in = jnp.dot(act_v[rs, cs], weights, preferred_element_type=jnp.float32)
            weights = out_v[:, :, cs].reshape(draws * k_out, cs.stop - cs.start)
            term_out = lax.dot_general(
                grad_v[rs, cs], weights, (((1,), (1,)), ((), ())), preferred_element_type=jnp.float32
            )
            sums = (term_in, term_out) if sums is None else (sums[0] + term_in, sums[1] + term_out)
        return sums

    def factors(sums):
        low_in = sums[0].astype(jnp.bfloat16)
        found = []
        for e in range(part_count):
            ts = slice(e * length, (e + 1) * length)
            lhs = jnp.concatenate([sums[1][ts, i * k_out:(i + 1) * k_out] for i in range(draws)], axis=0)
            rhs = jnp.concatenate([low_in[ts, i * k_in:(i + 1) * k_in] for i in range(draws)], axis=0)
            found.append((lhs.T.astype(jnp.bfloat16), rhs))
        return found

    def terms(found, which, p, into):
        for e, (lhs, rhs) in enumerate(found):
            lhs = jnp.where(which == 0, lhs[:k_half], lhs[k_half:])
            into[p, pl.ds(e, k_half, stride=part_count), :] = jnp.dot(lhs, rhs, preferred_element_type=jnp.float32)

    def remote(src, dst, ssem, rsem, section, dp):
        return pltpu.make_async_remote_copy(
            src_ref=src, dst_ref=dst, send_sem=ssem, recv_sem=rsem,
            device_id={"section": section, "dp": dp}, device_id_type=MESH,
        )

    def across(c, i):
        bit = 1
        while bit < chips:
            if i & bit:
                c = c + bit * (1 - 2 * ((c // bit) % 2))
            bit *= 2
        return c

    k_chunk = k_half // chips
    rows = k_chunk * part_count
    turns = [2 * (m ^ m // 2) + b for m in range(1, chips // 2) for b in (0, 1)] + [1]

    def chunk(c):
        return pl.ds(pl.multiple_of(c * rows, rows), rows)

    def swap(p):
        return remote(theirs.at[p], arrived.at[p], send_sem.at[4], pair_sem.at[p], partner, d)

    def scatter(p):
        for slot, i in enumerate(turns):
            to = across(chip, i)
            ks = chunk(to)
            mine[p, ks, :] = mine[p, ks, :] + arrived[p, ks, :]
            remote(mine.at[p, ks], pieces.at[p, slot], send_sem.at[0], recv_sem.at[p], 2 * to + core, d).start()

    sums = []
    for p in range(parts):
        late = p == parts - 1
        early = spans[p][:TURN] if late else spans[p]
        total = project(p, early, None)
        if late:
            pl.semaphore_wait(barrier, n * groups)
            for o in range(p):
                swap(o).start()
            total = project(p, spans[p][TURN:], total)
        found = factors(total)
        terms(found, 1 - core, p, theirs)
        if late:
            swap(p).start()
            for o in range(p):
                swap(o).wait_recv()
                scatter(o)
        terms(found, core, p, mine)
    swap(parts - 1).wait_recv()
    scatter(parts - 1)
    hold = pltpu.make_async_copy(earlier, held, held_sem)
    hold.start()

    per_group = n // groups
    q = core * chips + chip
    own_slot = q % per_group
    home = q // per_group
    at_home = home == d

    cross = jnp.logical_not(at_home)

    def gather(p):
        ps = pl.ds(p * rows, rows)

        def col_copy(to):
            return remote(own.at[ps], cols.at[own_slot, d, ps], send_sem.at[1], col_recv.at[own_slot], to, home)

        for i in range(chips - 1):
            col_copy(2 * jnp.where(chip <= i, i + 1, i) + core).start()

        @pl.when(at_home)
        def _():
            col_copy(partner).start()
            cols[own_slot, d, ps] = own[ps]

        @pl.when(cross)
        def _():
            col_copy(s).start()

        for g in range(groups):
            here = jnp.logical_and(q == s, d == g)

            @pl.when(jnp.logical_and(home != g, jnp.logical_not(here)))
            def _():
                remote(own.at[ps], row.at[d, ps], row_send.at[g], row_recv.at[d], q, g).start()

            @pl.when(jnp.logical_and(home != g, here))
            def _():
                row[d, ps] = own[ps]

    for p in range(parts):
        ks = chunk(chip)
        total = mine[p, ks, :] + arrived[p, ks, :]
        remote(pieces.at[p], pieces.at[p], send_sem.at[0], recv_sem.at[p], partner, d).wait_recv()
        for i in range(chips - 1):
            total = total + pieces[p, i]
        own[p * rows:(p + 1) * rows, :] = total
        gather(p)

    def rows_of(ref, k):
        starts = [p * rows + k * part_count for p in range(parts)]
        return jnp.concatenate([ref[g, at:at + part_count] for g in range(groups) for at in starts], axis=0)

    def forward(j, lo, size, sem):
        ref = cols.at[j, pl.ds(lo, size)]
        return remote(ref, ref, send_sem.at[sem], col_recv.at[j], partner, d)

    passes = d * per_group // chips == core
    for i in range(per_group):
        j = across(chip, i) % per_group
        mixed = d * per_group + j == q

        @pl.when(jnp.logical_not(mixed))
        def _():
            forward(j, 0, groups, 2).wait_recv()

            @pl.when(passes)
            def _():
                forward(j, 0, groups, 2).start()

        @pl.when(mixed)
        def _():
            forward(j, 0, groups - 1, 3).wait_recv()
            for g in range(groups):

                @pl.when(d != g)
                def _():
                    forward(j, g, 1, 3).start()

        for k in range(k_chunk):
            hi, lo = split(rows_of(cols.at[j], k))
            at = pl.multiple_of((j * k_chunk + k) * LANES, LANES)
            right[:, pl.ds(at, LANES)] = jnp.concatenate([hi, hi, lo], axis=0)

    for g in range(groups):

        @pl.when(jnp.logical_and(s // per_group != d, jnp.logical_or(q != s, d != g)))
        def _():
            remote(own, row.at[g], row_send.at[g], row_recv.at[g], q, d).wait_recv()

    @pl.when(s // per_group == d)
    def _():
        row[...] = cols[s % per_group]

    for k in range(k_chunk):
        hi, lo = split(rows_of(row, k) * scale)
        left[:, k * LANES:(k + 1) * LANES] = jnp.concatenate([hi, lo, hi], axis=0)

    hold.wait()
    remote(theirs, theirs, send_sem.at[4], recv_sem.at[0], partner, d).wait_send()
    remote(pieces, pieces, send_sem.at[0], recv_sem.at[0], partner, d).wait_send()
    remote(arrived, arrived, send_sem.at[1], recv_sem.at[0], partner, d).wait_send()
    for g in range(groups):

        @pl.when(jnp.logical_and(home != g, jnp.logical_or(q != s, d != g)))
        def _():
            remote(own, row.at[d], row_send.at[g], row_recv.at[d], q, g).wait_send()

    def forwarded(count, sem):
        ref = cols.at[pl.ds(0, count)]
        remote(ref, ref, send_sem.at[sem], recv_sem.at[0], partner, d).wait_send()

    @pl.when(at_home)
    def _():
        forwarded(per_group - 1, 2)
        forward(0, 0, groups - 1, 3).wait_send()

    @pl.when(jnp.logical_and(passes, cross))
    def _():
        forwarded(per_group, 2)


def gram_kernel(tiles, left, right, earlier, out, tile_v, sem):
    height = earlier.shape[0] // tiles
    lhs = left[...].T
    copies = []
    for i in range(tiles):
        rs = slice(i * height, (i + 1) * height)
        tile_v[rs, :] = earlier[rs, :] + jnp.dot(lhs[rs], right[...], preferred_element_type=jnp.float32)
        copy = pltpu.make_async_copy(
            tile_v.at[pl.ds(i * height, height)], out.at[pl.ds(i * height, height)], sem.at[0]
        )
        copy.start()
        copies.append(copy)
    pltpu.make_async_copy(tile_v, out, sem.at[0]).wait()


def per_device(activations, out_grads, proj_in, proj_out, earlier_gram):
    n = lax.axis_size("section")
    groups = lax.axis_size("dp")
    _, count, length, width = activations.shape
    _, draws, _, k_in = proj_in.shape
    k_out = proj_out.shape[2]
    tokens = count * length
    examples = count * groups
    scale = 1.0 / (length * n * draws) / examples
    row_width, col_width = earlier_gram.shape
    chips = n // 2
    k_half = k_out // 2
    k_chunk = k_half // chips
    per_group = n // groups
    parts = len(PIECES)
    half_rows = k_half * (count // parts)
    rows = half_rows // chips
    any_spec = pl.BlockSpec(memory_space=pl.ANY)
    vmem_spec = pl.BlockSpec(memory_space=pltpu.VMEM)
    f32, bf16 = jnp.float32, jnp.bfloat16
    dma = pltpu.SemaphoreType.DMA

    left, right, held = pl.pallas_call(
        functools.partial(feature_kernel, n, groups, count, scale),
        out_shape=(
            pltpu.VMEM((3 * examples, row_width), bf16),
            pltpu.VMEM((3 * examples, col_width), bf16),
            pltpu.VMEM((row_width, col_width), f32),
        ),
        in_specs=[any_spec] * 5,
        out_specs=(vmem_spec, vmem_spec, vmem_spec),
        scratch_shapes=[
            pltpu.VMEM((tokens, width), bf16),
            pltpu.VMEM((tokens, width), bf16),
            pltpu.VMEM((draws, width, k_in), bf16),
            pltpu.VMEM((draws, k_out, width), bf16),
            pltpu.VMEM((parts, half_rows, k_in), f32),
            pltpu.VMEM((parts, half_rows, k_in), f32),
            pltpu.VMEM((parts, half_rows, k_in), f32),
            pltpu.VMEM((parts, chips - 1, rows, k_in), f32),
            pltpu.VMEM((parts * rows, k_in), f32),
            pltpu.VMEM((per_group, groups, parts * rows, k_in), f32),
            pltpu.VMEM((groups, parts * rows, k_in), f32),
            dma((sum(len(shares) for shares in PIECES),)),
            dma((parts,)),
            dma((5,)),
            dma((parts,)),
            dma((per_group,)),
            dma((groups,)),
            dma((groups,)),
            dma,
        ],
        compiler_params=pltpu.CompilerParams(
            collective_id=0, has_side_effects=True, vmem_limit_bytes=52 << 20
        ),
        name="features",
    )(
        activations.reshape(tokens, width),
        out_grads.reshape(tokens, width),
        proj_in[0],
        proj_out[0],
        earlier_gram,
    )
    tiles = 16
    return pl.pallas_call(
        functools.partial(gram_kernel, tiles),
        out_shape=jax.ShapeDtypeStruct((row_width, col_width), f32),
        in_specs=[vmem_spec, vmem_spec, vmem_spec],
        out_specs=any_spec,
        scratch_shapes=[pltpu.VMEM((row_width, col_width), f32), dma((1,))],
        compiler_params=pltpu.CompilerParams(vmem_limit_bytes=28 << 20),
        name="gram",
    )(left, right, held)


def solution(mesh):
    return jax.shard_map(
        per_device,
        mesh=mesh,
        in_specs=(
            P("section", "dp", None, None),
            P("section", "dp", None, None),
            P("section", None, None, None),
            P("section", None, None, None),
            P("section", "dp"),
        ),
        out_specs=P("section", "dp"),
        check_vma=False,
    )
```

```python
import functools
import math

import jax
import jax.numpy as jnp
from jax import lax
from jax.experimental import pallas as pl
from jax.experimental.pallas import tpu as pltpu
from jax.sharding import PartitionSpec as P

MESH = pl.DeviceIdType.MESH
LANES = 128
PIECES = ((2, 2, 2, 2), (2, 2, 2, 2))
FIRST = 2
TURN = 1


def split(x):
    hi = x.astype(jnp.bfloat16)
    lo = (x - hi.astype(jnp.float32)).astype(jnp.bfloat16)
    return hi, lo


def feature_kernel(
    n, groups, count, scale,
    act, grad, p_in, p_out, earlier,
    left, right, held,
    act_v, grad_v, in_v, out_v,
    theirs, mine, arrived, pieces, own, cols, row,
    load_sem, pair_sem, send_sem, recv_sem, col_recv, row_send, row_recv, held_sem,
):
    s = lax.axis_index("section")
    d = lax.axis_index("dp")
    chips = n // 2
    core = s % 2
    chip = s // 2
    partner = s + 1 - 2 * core

    draws, width, k_in = p_in.shape
    k_out = p_out.shape[1]
    tokens = act.shape[0]
    length = tokens // count

    parts = len(PIECES)
    part_count = count // parts
    part_tokens = part_count * length
    k_half = k_out // 2
    half_rows = k_half * part_count

    loads, spans = [], []
    for p, shares in enumerate(PIECES):
        rs = slice(p * part_tokens, (p + 1) * part_tokens)
        spans.append([])
        at = 0
        for share in shares:
            depth = width * share // sum(shares)
            cs = slice(at, at + depth)
            at += depth
            sem = load_sem.at[len(loads)]
            copies = []
            if p == 0:
                copies.append(pltpu.make_async_copy(p_in.at[:, cs], in_v.at[:, cs], sem))
                copies.append(pltpu.make_async_copy(p_out.at[:, :, cs], out_v.at[:, :, cs], sem))
            copies.append(pltpu.make_async_copy(act.at[rs, cs], act_v.at[rs, cs], sem))
            copies.append(pltpu.make_async_copy(grad.at[rs, cs], grad_v.at[rs, cs], sem))
            taken = depth * (2 * part_tokens + (draws * (k_in + k_out) if p == 0 else 0)) // width
            whole = pltpu.make_async_copy(act.at[pl.ds(0, taken)], act_v.at[pl.ds(0, taken)], sem)
            spans[p].append((cs, whole))
            loads.append(copies)

    def start(some):
        for copies in some:
            for copy in copies:
                copy.start()

    start(loads[:FIRST])
    barrier = pltpu.get_barrier_semaphore()
    for g in range(groups):
        for i in range(n):
            pl.semaphore_signal(barrier, inc=1, device_id={"section": i, "dp": g}, device_id_type=MESH)
    start(loads[FIRST:])

    def project(p, pieces_now, sums):
        rs = slice(p * part_tokens, (p + 1) * part_tokens)
        for cs, whole in pieces_now:
            whole.wait()
            weights = jnp.concatenate([in_v[i, cs, :] for i in range(draws)], axis=1)
            term_in = jnp.dot(act_v[rs, cs], weights, preferred_element_type=jnp.float32)
            weights = out_v[:, :, cs].reshape(draws * k_out, cs.stop - cs.start)
            term_out = lax.dot_general(
                grad_v[rs, cs], weights, (((1,), (1,)), ((), ())), preferred_element_type=jnp.float32
            )
            sums = (term_in, term_out) if sums is None else (sums[0] + term_in, sums[1] + term_out)
        return sums

    def factors(sums):
        low_in = sums[0].astype(jnp.bfloat16)
        found = []
        for e in range(part_count):
            ts = slice(e * length, (e + 1) * length)
            lhs = jnp.concatenate([sums[1][ts, i * k_out:(i + 1) * k_out] for i in range(draws)], axis=0)
            rhs = jnp.concatenate([low_in[ts, i * k_in:(i + 1) * k_in] for i in range(draws)], axis=0)
            found.append((lhs.T.astype(jnp.bfloat16), rhs))
        return found

    def terms(found, which, p, into):
        for e, (lhs, rhs) in enumerate(found):
            lhs = jnp.where(which == 0, lhs[:k_half], lhs[k_half:])
            into[p, pl.ds(e, k_half, stride=part_count), :] = jnp.dot(lhs, rhs, preferred_element_type=jnp.float32)

    def remote(src, dst, ssem, rsem, section, dp):
        return pltpu.make_async_remote_copy(
            src_ref=src, dst_ref=dst, send_sem=ssem, recv_sem=rsem,
            device_id={"section": section, "dp": dp}, device_id_type=MESH,
        )

    def across(c, i):
        bit = 1
        while bit < chips:
            if i & bit:
                c = c + bit * (1 - 2 * ((c // bit) % 2))
            bit *= 2
        return c

    k_chunk = k_half // chips
    rows = k_chunk * part_count
    turns = [2 * (m ^ m // 2) + b for m in range(1, chips // 2) for b in (0, 1)] + [1]

    def chunk(c):
        return pl.ds(pl.multiple_of(c * rows, rows), rows)

    def swap(p):
        return remote(theirs.at[p], arrived.at[p], send_sem.at[4], pair_sem.at[p], partner, d)

    def scatter(p):
        for slot, i in enumerate(turns):
            to = across(chip, i)
            ks = chunk(to)
            mine[p, ks, :] = mine[p, ks, :] + arrived[p, ks, :]
            remote(mine.at[p, ks], pieces.at[p, slot], send_sem.at[0], recv_sem.at[p], 2 * to + core, d).start()

    sums = []
    for p in range(parts):
        late = p == parts - 1
        early = spans[p][:TURN] if late else spans[p]
        total = project(p, early, None)
        if late:
            pl.semaphore_wait(barrier, n * groups)
            for o in range(p):
                swap(o).start()
            total = project(p, spans[p][TURN:], total)
        found = factors(total)
        terms(found, 1 - core, p, theirs)
        if late:
            swap(p).start()
            for o in range(p):
                swap(o).wait_recv()
                scatter(o)
        terms(found, core, p, mine)
    swap(parts - 1).wait_recv()
    scatter(parts - 1)
    hold = pltpu.make_async_copy(earlier, held, held_sem)
    hold.start()

    per_group = n // groups
    q = core * chips + chip
    own_slot = q % per_group
    home = q // per_group
    at_home = home == d

    cross = jnp.logical_not(at_home)
    direct = jnp.logical_and(chip == 0, d == 0)
    twice = jnp.logical_and(home == 0, jnp.logical_not(direct))

    def gather(p):
        ps = pl.ds(p * rows, rows)

        def col_copy(to):
            return remote(own.at[ps], cols.at[own_slot, d, ps], send_sem.at[1], col_recv.at[own_slot], to, home)

        for i in range(chips):
            col_copy(jnp.where(jnp.logical_and(at_home, chip == i), partner, 2 * i + core)).start()
            if i == 0:

                @pl.when(twice)
                def _():
                    remote(
                        own.at[ps], cols.at[own_slot, d, ps], send_sem.at[5], col_recv.at[own_slot], 1 - core, home
                    ).start()

        @pl.when(at_home)
        def _():
            cols[own_slot, d, ps] = own[ps]

        for g in range(groups):
            here = jnp.logical_and(q == s, d == g)

            @pl.when(jnp.logical_and(home != g, jnp.logical_not(here)))
            def _():
                remote(own.at[ps], row.at[d, ps], row_send.at[g], row_recv.at[d], q, g).start()

            @pl.when(jnp.logical_and(home != g, here))
            def _():
                row[d, ps] = own[ps]

    for p in range(parts):
        ks = chunk(chip)
        total = mine[p, ks, :] + arrived[p, ks, :]
        remote(pieces.at[p], pieces.at[p], send_sem.at[0], recv_sem.at[p], partner, d).wait_recv()
        for i in range(chips - 1):
            total = total + pieces[p, i]
        own[p * rows:(p + 1) * rows, :] = total
        gather(p)

    def rows_of(ref, k):
        starts = [p * rows + k * part_count for p in range(parts)]
        return jnp.concatenate([ref[g, at:at + part_count] for g in range(groups) for at in starts], axis=0)

    def forward(j, lo, size, sem):
        ref = cols.at[j, pl.ds(lo, size)]
        return remote(ref, ref, send_sem.at[sem], col_recv.at[j], partner, d)

    passes = jnp.logical_and(d * per_group // chips == core, jnp.logical_not(direct))
    for i in range(per_group):
        j = across(chip, i) % per_group
        mixed = d * per_group + j == q

        @pl.when(jnp.logical_not(mixed))
        def _():
            forward(j, 0, groups, 2).wait_recv()

            @pl.when(passes)
            def _():
                forward(j, 0, groups, 2).start()

        @pl.when(mixed)
        def _():
            forward(j, 0, groups - 1, 3).wait_recv()
            for g in range(groups):

                @pl.when(jnp.logical_and(passes, d != g))
                def _():
                    forward(j, g, 1, 3).start()

        for k in range(k_chunk):
            hi, lo = split(rows_of(cols.at[j], k))
            at = pl.multiple_of((j * k_chunk + k) * LANES, LANES)
            right[:, pl.ds(at, LANES)] = jnp.concatenate([hi, hi, lo], axis=0)

    for g in range(groups):

        @pl.when(jnp.logical_and(s // per_group != d, jnp.logical_or(q != s, d != g)))
        def _():
            remote(own, row.at[g], row_send.at[g], row_recv.at[g], q, d).wait_recv()

    @pl.when(s // per_group == d)
    def _():
        row[...] = cols[s % per_group]

    for k in range(k_chunk):
        hi, lo = split(rows_of(row, k) * scale)
        left[:, k * LANES:(k + 1) * LANES] = jnp.concatenate([hi, lo, hi], axis=0)

    hold.wait()
    remote(theirs, theirs, send_sem.at[4], recv_sem.at[0], partner, d).wait_send()
    remote(pieces, pieces, send_sem.at[0], recv_sem.at[0], partner, d).wait_send()
    remote(arrived, arrived, send_sem.at[1], recv_sem.at[0], partner, d).wait_send()
    for g in range(groups):

        @pl.when(jnp.logical_and(home != g, jnp.logical_or(q != s, d != g)))
        def _():
            remote(own, row.at[d], row_send.at[g], row_recv.at[d], q, g).wait_send()

    def forwarded(count, sem):
        ref = cols.at[pl.ds(0, count)]
        remote(ref, ref, send_sem.at[sem], recv_sem.at[0], partner, d).wait_send()

    @pl.when(twice)
    def _():
        remote(own, own, send_sem.at[5], recv_sem.at[0], partner, d).wait_send()

    @pl.when(jnp.logical_and(passes, at_home))
    def _():
        forwarded(per_group - 1, 2)
        forward(0, 0, groups - 1, 3).wait_send()

    @pl.when(jnp.logical_and(passes, cross))
    def _():
        forwarded(per_group, 2)


def gram_kernel(tiles, left, right, earlier, out, tile_v, sem):
    height = earlier.shape[0] // tiles
    lhs = left[...].T
    copies = []
    for i in range(tiles):
        rs = slice(i * height, (i + 1) * height)
        tile_v[rs, :] = earlier[rs, :] + jnp.dot(lhs[rs], right[...], preferred_element_type=jnp.float32)
        copy = pltpu.make_async_copy(
            tile_v.at[pl.ds(i * height, height)], out.at[pl.ds(i * height, height)], sem.at[0]
        )
        copy.start()
        copies.append(copy)
    pltpu.make_async_copy(tile_v, out, sem.at[0]).wait()


def per_device(activations, out_grads, proj_in, proj_out, earlier_gram):
    n = lax.axis_size("section")
    groups = lax.axis_size("dp")
    _, count, length, width = activations.shape
    _, draws, _, k_in = proj_in.shape
    k_out = proj_out.shape[2]
    tokens = count * length
    examples = count * groups
    scale = 1.0 / (length * n * draws) / examples
    row_width, col_width = earlier_gram.shape
    chips = n // 2
    k_half = k_out // 2
    k_chunk = k_half // chips
    per_group = n // groups
    parts = len(PIECES)
    half_rows = k_half * (count // parts)
    rows = half_rows // chips
    any_spec = pl.BlockSpec(memory_space=pl.ANY)
    vmem_spec = pl.BlockSpec(memory_space=pltpu.VMEM)
    f32, bf16 = jnp.float32, jnp.bfloat16
    dma = pltpu.SemaphoreType.DMA

    left, right, held = pl.pallas_call(
        functools.partial(feature_kernel, n, groups, count, scale),
        out_shape=(
            pltpu.VMEM((3 * examples, row_width), bf16),
            pltpu.VMEM((3 * examples, col_width), bf16),
            pltpu.VMEM((row_width, col_width), f32),
        ),
        in_specs=[any_spec] * 5,
        out_specs=(vmem_spec, vmem_spec, vmem_spec),
        scratch_shapes=[
            pltpu.VMEM((tokens, width), bf16),
            pltpu.VMEM((tokens, width), bf16),
            pltpu.VMEM((draws, width, k_in), bf16),
            pltpu.VMEM((draws, k_out, width), bf16),
            pltpu.VMEM((parts, half_rows, k_in), f32),
            pltpu.VMEM((parts, half_rows, k_in), f32),
            pltpu.VMEM((parts, half_rows, k_in), f32),
            pltpu.VMEM((parts, chips - 1, rows, k_in), f32),
            pltpu.VMEM((parts * rows, k_in), f32),
            pltpu.VMEM((per_group, groups, parts * rows, k_in), f32),
            pltpu.VMEM((groups, parts * rows, k_in), f32),
            dma((sum(len(shares) for shares in PIECES),)),
            dma((parts,)),
            dma((6,)),
            dma((parts,)),
            dma((per_group,)),
            dma((groups,)),
            dma((groups,)),
            dma,
        ],
        compiler_params=pltpu.CompilerParams(
            collective_id=0, has_side_effects=True, vmem_limit_bytes=52 << 20
        ),
        name="features",
    )(
        activations.reshape(tokens, width),
        out_grads.reshape(tokens, width),
        proj_in[0],
        proj_out[0],
        earlier_gram,
    )
    tiles = 16
    return pl.pallas_call(
        functools.partial(gram_kernel, tiles),
        out_shape=jax.ShapeDtypeStruct((row_width, col_width), f32),
        in_specs=[vmem_spec, vmem_spec, vmem_spec],
        out_specs=any_spec,
        scratch_shapes=[pltpu.VMEM((row_width, col_width), f32), dma((1,))],
        compiler_params=pltpu.CompilerParams(vmem_limit_bytes=28 << 20),
        name="gram",
    )(left, right, held)


def solution(mesh):
    return jax.shard_map(
        per_device,
        mesh=mesh,
        in_specs=(
            P("section", "dp", None, None),
            P("section", "dp", None, None),
            P("section", None, None, None),
            P("section", None, None, None),
            P("section", "dp"),
        ),
        out_specs=P("section", "dp"),
        check_vma=False,
    )
```

```python
import functools
import math

import jax
import jax.numpy as jnp
from jax import lax
from jax.experimental import pallas as pl
from jax.experimental.pallas import tpu as pltpu
from jax.sharding import PartitionSpec as P

MESH = pl.DeviceIdType.MESH
LANES = 128
PIECES = ((2, 2, 2, 2), (2, 2, 2, 2))
FIRST = 2
TURN = 1
TILES = (1, 1, 2, 4, 4, 4, 4, 4, 4, 2, 1, 1)


def split(x):
    hi = x.astype(jnp.bfloat16)
    lo = (x - hi.astype(jnp.float32)).astype(jnp.bfloat16)
    return hi, lo


def feature_kernel(
    n, groups, count, scale,
    act, grad, p_in, p_out, earlier,
    left, right, held,
    act_v, grad_v, in_v, out_v,
    theirs, mine, arrived, pieces, own, cols, row,
    load_sem, pair_sem, send_sem, recv_sem, col_recv, row_send, row_recv, held_sem,
):
    s = lax.axis_index("section")
    d = lax.axis_index("dp")
    chips = n // 2
    core = s % 2
    chip = s // 2
    partner = s + 1 - 2 * core

    draws, width, k_in = p_in.shape
    k_out = p_out.shape[1]
    tokens = act.shape[0]
    length = tokens // count

    parts = len(PIECES)
    part_count = count // parts
    part_tokens = part_count * length
    k_half = k_out // 2
    half_rows = k_half * part_count

    loads, spans = [], []
    for p, shares in enumerate(PIECES):
        rs = slice(p * part_tokens, (p + 1) * part_tokens)
        spans.append([])
        at = 0
        for share in shares:
            depth = width * share // sum(shares)
            cs = slice(at, at + depth)
            at += depth
            sem = load_sem.at[len(loads)]
            copies = []
            if p == 0:
                copies.append(pltpu.make_async_copy(p_in.at[:, cs], in_v.at[:, cs], sem))
                copies.append(pltpu.make_async_copy(p_out.at[:, :, cs], out_v.at[:, :, cs], sem))
            copies.append(pltpu.make_async_copy(act.at[rs, cs], act_v.at[rs, cs], sem))
            copies.append(pltpu.make_async_copy(grad.at[rs, cs], grad_v.at[rs, cs], sem))
            taken = depth * (2 * part_tokens + (draws * (k_in + k_out) if p == 0 else 0)) // width
            whole = pltpu.make_async_copy(act.at[pl.ds(0, taken)], act_v.at[pl.ds(0, taken)], sem)
            spans[p].append((cs, whole))
            loads.append(copies)

    def start(some):
        for copies in some:
            for copy in copies:
                copy.start()

    start(loads[:FIRST])
    barrier = pltpu.get_barrier_semaphore()
    for g in range(groups):
        for i in range(n):
            pl.semaphore_signal(barrier, inc=1, device_id={"section": i, "dp": g}, device_id_type=MESH)
    start(loads[FIRST:])

    def project(p, pieces_now, sums):
        rs = slice(p * part_tokens, (p + 1) * part_tokens)
        for cs, whole in pieces_now:
            whole.wait()
            weights = jnp.concatenate([in_v[i, cs, :] for i in range(draws)], axis=1)
            term_in = jnp.dot(act_v[rs, cs], weights, preferred_element_type=jnp.float32)
            weights = out_v[:, :, cs].reshape(draws * k_out, cs.stop - cs.start)
            term_out = lax.dot_general(
                grad_v[rs, cs], weights, (((1,), (1,)), ((), ())), preferred_element_type=jnp.float32
            )
            sums = (term_in, term_out) if sums is None else (sums[0] + term_in, sums[1] + term_out)
        return sums

    def factors(sums):
        low_in = sums[0].astype(jnp.bfloat16)
        found = []
        for e in range(part_count):
            ts = slice(e * length, (e + 1) * length)
            lhs = jnp.concatenate([sums[1][ts, i * k_out:(i + 1) * k_out] for i in range(draws)], axis=0)
            rhs = jnp.concatenate([low_in[ts, i * k_in:(i + 1) * k_in] for i in range(draws)], axis=0)
            found.append((lhs.T.astype(jnp.bfloat16), rhs))
        return found

    def terms(found, which, p, into):
        for e, (lhs, rhs) in enumerate(found):
            lhs = jnp.where(which == 0, lhs[:k_half], lhs[k_half:])
            into[p, pl.ds(e, k_half, stride=part_count), :] = jnp.dot(lhs, rhs, preferred_element_type=jnp.float32)

    def remote(src, dst, ssem, rsem, section, dp):
        return pltpu.make_async_remote_copy(
            src_ref=src, dst_ref=dst, send_sem=ssem, recv_sem=rsem,
            device_id={"section": section, "dp": dp}, device_id_type=MESH,
        )

    def across(c, i):
        bit = 1
        while bit < chips:
            if i & bit:
                c = c + bit * (1 - 2 * ((c // bit) % 2))
            bit *= 2
        return c

    k_chunk = k_half // chips
    rows = k_chunk * part_count
    turns = [2 * (m ^ m // 2) + b for m in range(1, chips // 2) for b in (0, 1)] + [1]

    def chunk(c):
        return pl.ds(pl.multiple_of(c * rows, rows), rows)

    def swap(p):
        return remote(theirs.at[p], arrived.at[p], send_sem.at[4], pair_sem.at[p], partner, d)

    def scatter(p):
        for slot, i in enumerate(turns):
            to = across(chip, i)
            ks = chunk(to)
            mine[p, ks, :] = mine[p, ks, :] + arrived[p, ks, :]
            remote(mine.at[p, ks], pieces.at[p, slot], send_sem.at[0], recv_sem.at[p], 2 * to + core, d).start()

    sums = []
    for p in range(parts):
        late = p == parts - 1
        early = spans[p][:TURN] if late else spans[p]
        total = project(p, early, None)
        if late:
            pl.semaphore_wait(barrier, n * groups)
            for o in range(p):
                swap(o).start()
            total = project(p, spans[p][TURN:], total)
        found = factors(total)
        terms(found, 1 - core, p, theirs)
        if late:
            swap(p).start()
            for o in range(p):
                swap(o).wait_recv()
                scatter(o)
        terms(found, core, p, mine)
    swap(parts - 1).wait_recv()
    scatter(parts - 1)
    hold = pltpu.make_async_copy(earlier, held, held_sem)
    hold.start()

    per_group = n // groups
    q = core * chips + chip
    own_slot = q % per_group
    home = q // per_group
    at_home = home == d

    cross = jnp.logical_not(at_home)
    direct = jnp.logical_and(chip == 0, d == 0)
    twice = jnp.logical_and(home == 0, jnp.logical_not(direct))

    def gather(p):
        ps = pl.ds(p * rows, rows)

        def col_copy(to):
            return remote(own.at[ps], cols.at[own_slot, d, ps], send_sem.at[1], col_recv.at[own_slot], to, home)

        for i in range(chips):
            to = jnp.where(core == 0, i, chips - 1 - i)
            col_copy(jnp.where(jnp.logical_and(at_home, chip == to), partner, 2 * to + core)).start()
            if i == 1:

                @pl.when(twice)
                def _():
                    remote(
                        own.at[ps], cols.at[own_slot, d, ps], send_sem.at[5], col_recv.at[own_slot], 1 - core, home
                    ).start()

        @pl.when(at_home)
        def _():
            cols[own_slot, d, ps] = own[ps]

        for g in range(groups):
            here = jnp.logical_and(q == s, d == g)

            @pl.when(jnp.logical_and(home != g, jnp.logical_not(here)))
            def _():
                remote(own.at[ps], row.at[d, ps], row_send.at[g], row_recv.at[d], q, g).start()

            @pl.when(jnp.logical_and(home != g, here))
            def _():
                row[d, ps] = own[ps]

    for p in range(parts):
        ks = chunk(chip)
        total = mine[p, ks, :] + arrived[p, ks, :]
        remote(pieces.at[p], pieces.at[p], send_sem.at[0], recv_sem.at[p], partner, d).wait_recv()
        for i in range(chips - 1):
            total = total + pieces[p, i]
        own[p * rows:(p + 1) * rows, :] = total
        gather(p)

    def rows_of(ref, k):
        starts = [p * rows + k * part_count for p in range(parts)]
        return jnp.concatenate([ref[g, at:at + part_count] for g in range(groups) for at in starts], axis=0)

    def forward(j, lo, size, sem):
        ref = cols.at[j, pl.ds(lo, size)]
        return remote(ref, ref, send_sem.at[sem], col_recv.at[j], partner, d)

    passes = jnp.logical_and(d * per_group // chips == core, jnp.logical_not(direct))
    for i in range(per_group):
        j = across(chip, i) % per_group
        mixed = d * per_group + j == q

        @pl.when(jnp.logical_not(mixed))
        def _():
            forward(j, 0, groups, 2).wait_recv()

            @pl.when(passes)
            def _():
                forward(j, 0, groups, 2).start()

        @pl.when(mixed)
        def _():
            forward(j, 0, groups - 1, 3).wait_recv()
            for g in range(groups):

                @pl.when(jnp.logical_and(passes, d != g))
                def _():
                    forward(j, g, 1, 3).start()

        for k in range(k_chunk):
            hi, lo = split(rows_of(cols.at[j], k))
            at = pl.multiple_of((j * k_chunk + k) * LANES, LANES)
            right[:, pl.ds(at, LANES)] = jnp.concatenate([hi, hi, lo], axis=0)

    for g in range(groups):

        @pl.when(jnp.logical_and(s // per_group != d, jnp.logical_or(q != s, d != g)))
        def _():
            remote(own, row.at[g], row_send.at[g], row_recv.at[g], q, d).wait_recv()

    @pl.when(s // per_group == d)
    def _():
        row[...] = cols[s % per_group]

    for k in range(k_chunk):
        hi, lo = split(rows_of(row, k) * scale)
        left[:, k * LANES:(k + 1) * LANES] = jnp.concatenate([hi, lo, hi], axis=0)

    hold.wait()
    remote(theirs, theirs, send_sem.at[4], recv_sem.at[0], partner, d).wait_send()
    remote(pieces, pieces, send_sem.at[0], recv_sem.at[0], partner, d).wait_send()
    remote(arrived, arrived, send_sem.at[1], recv_sem.at[0], partner, d).wait_send()
    for g in range(groups):

        @pl.when(jnp.logical_and(home != g, jnp.logical_or(q != s, d != g)))
        def _():
            remote(own, row.at[d], row_send.at[g], row_recv.at[d], q, g).wait_send()

    def forwarded(count, sem):
        ref = cols.at[pl.ds(0, count)]
        remote(ref, ref, send_sem.at[sem], recv_sem.at[0], partner, d).wait_send()

    @pl.when(twice)
    def _():
        remote(own, own, send_sem.at[5], recv_sem.at[0], partner, d).wait_send()

    @pl.when(jnp.logical_and(passes, at_home))
    def _():
        forwarded(per_group - 1, 2)
        forward(0, 0, groups - 1, 3).wait_send()

    @pl.when(jnp.logical_and(passes, cross))
    def _():
        forwarded(per_group, 2)


def gram_kernel(left, right, earlier, out, tile_v, sem):
    lhs = left[...].T
    at = 0
    for share in TILES:
        height = earlier.shape[0] * share // sum(TILES)
        rs = slice(at, at + height)
        tile_v[rs, :] = earlier[rs, :] + jnp.dot(lhs[rs], right[...], preferred_element_type=jnp.float32)
        pltpu.make_async_copy(tile_v.at[rs], out.at[rs], sem).start()
        at += height
    pltpu.make_async_copy(tile_v, out, sem).wait()


def per_device(activations, out_grads, proj_in, proj_out, earlier_gram):
    n = lax.axis_size("section")
    groups = lax.axis_size("dp")
    _, count, length, width = activations.shape
    _, draws, _, k_in = proj_in.shape
    k_out = proj_out.shape[2]
    tokens = count * length
    examples = count * groups
    scale = 1.0 / (length * n * draws) / examples
    row_width, col_width = earlier_gram.shape
    chips = n // 2
    k_half = k_out // 2
    k_chunk = k_half // chips
    per_group = n // groups
    parts = len(PIECES)
    half_rows = k_half * (count // parts)
    rows = half_rows // chips
    any_spec = pl.BlockSpec(memory_space=pl.ANY)
    vmem_spec = pl.BlockSpec(memory_space=pltpu.VMEM)
    f32, bf16 = jnp.float32, jnp.bfloat16
    dma = pltpu.SemaphoreType.DMA

    left, right, held = pl.pallas_call(
        functools.partial(feature_kernel, n, groups, count, scale),
        out_shape=(
            pltpu.VMEM((3 * examples, row_width), bf16),
            pltpu.VMEM((3 * examples, col_width), bf16),
            pltpu.VMEM((row_width, col_width), f32),
        ),
        in_specs=[any_spec] * 5,
        out_specs=(vmem_spec, vmem_spec, vmem_spec),
        scratch_shapes=[
            pltpu.VMEM((tokens, width), bf16),
            pltpu.VMEM((tokens, width), bf16),
            pltpu.VMEM((draws, width, k_in), bf16),
            pltpu.VMEM((draws, k_out, width), bf16),
            pltpu.VMEM((parts, half_rows, k_in), f32),
            pltpu.VMEM((parts, half_rows, k_in), f32),
            pltpu.VMEM((parts, half_rows, k_in), f32),
            pltpu.VMEM((parts, chips - 1, rows, k_in), f32),
            pltpu.VMEM((parts * rows, k_in), f32),
            pltpu.VMEM((per_group, groups, parts * rows, k_in), f32),
            pltpu.VMEM((groups, parts * rows, k_in), f32),
            dma((sum(len(shares) for shares in PIECES),)),
            dma((parts,)),
            dma((6,)),
            dma((parts,)),
            dma((per_group,)),
            dma((groups,)),
            dma((groups,)),
            dma,
        ],
        compiler_params=pltpu.CompilerParams(
            collective_id=0, has_side_effects=True, vmem_limit_bytes=52 << 20
        ),
        name="features",
    )(
        activations.reshape(tokens, width),
        out_grads.reshape(tokens, width),
        proj_in[0],
        proj_out[0],
        earlier_gram,
    )
    return pl.pallas_call(
        gram_kernel,
        out_shape=jax.ShapeDtypeStruct((row_width, col_width), f32),
        in_specs=[vmem_spec, vmem_spec, vmem_spec],
        out_specs=any_spec,
        scratch_shapes=[pltpu.VMEM((row_width, col_width), f32), dma],
        compiler_params=pltpu.CompilerParams(vmem_limit_bytes=28 << 20),
        name="gram",
    )(left, right, held)


def solution(mesh):
    return jax.shard_map(
        per_device,
        mesh=mesh,
        in_specs=(
            P("section", "dp", None, None),
            P("section", "dp", None, None),
            P("section", None, None, None),
            P("section", None, None, None),
            P("section", "dp"),
        ),
        out_specs=P("section", "dp"),
        check_vma=False,
    )
```

```python
import functools
import math

import jax
import jax.numpy as jnp
from jax import lax
from jax.experimental import pallas as pl
from jax.experimental.pallas import tpu as pltpu
from jax.sharding import PartitionSpec as P

MESH = pl.DeviceIdType.MESH
LANES = 128
PIECES = ((2, 2, 2, 2), (2, 2, 2, 2))
FIRST = 2
TURN = 1
TILES = (1, 1, 2, 4, 4, 4, 4, 4, 4, 2, 1, 1)


def split(x):
    hi = x.astype(jnp.bfloat16)
    lo = (x - hi.astype(jnp.float32)).astype(jnp.bfloat16)
    return hi, lo


def feature_kernel(
    n, groups, count, scale,
    act, grad, p_in, p_out, earlier,
    left, right, held,
    act_v, grad_v, in_v, out_v,
    theirs, mine, arrived, pieces, own, cols, row,
    load_sem, pair_sem, recv_sem, col_recv, row_send, row_recv, held_sem,
):
    s = lax.axis_index("section")
    d = lax.axis_index("dp")
    chips = n // 2
    core = s % 2
    chip = s // 2
    partner = s + 1 - 2 * core

    draws, width, k_in = p_in.shape
    k_out = p_out.shape[1]
    tokens = act.shape[0]
    length = tokens // count

    parts = len(PIECES)
    part_count = count // parts
    part_tokens = part_count * length
    k_half = k_out // 2
    half_rows = k_half * part_count

    loads, spans = [], []
    for p, shares in enumerate(PIECES):
        rs = slice(p * part_tokens, (p + 1) * part_tokens)
        spans.append([])
        at = 0
        for share in shares:
            depth = width * share // sum(shares)
            cs = slice(at, at + depth)
            at += depth
            sem = load_sem.at[len(loads)]
            copies = []
            if p == 0:
                copies.append(pltpu.make_async_copy(p_in.at[:, cs], in_v.at[:, cs], sem))
                copies.append(pltpu.make_async_copy(p_out.at[:, :, cs], out_v.at[:, :, cs], sem))
            copies.append(pltpu.make_async_copy(act.at[rs, cs], act_v.at[rs, cs], sem))
            copies.append(pltpu.make_async_copy(grad.at[rs, cs], grad_v.at[rs, cs], sem))
            taken = depth * (2 * part_tokens + (draws * (k_in + k_out) if p == 0 else 0)) // width
            whole = pltpu.make_async_copy(act.at[pl.ds(0, taken)], act_v.at[pl.ds(0, taken)], sem)
            spans[p].append((cs, whole))
            loads.append(copies)

    def start(some):
        for copies in some:
            for copy in copies:
                copy.start()

    start(loads[:FIRST])
    barrier = pltpu.get_barrier_semaphore()
    for g in range(groups):
        for i in range(n):
            pl.semaphore_signal(barrier, inc=1, device_id={"section": i, "dp": g}, device_id_type=MESH)
    start(loads[FIRST:])

    def project(p, pieces_now, sums):
        rs = slice(p * part_tokens, (p + 1) * part_tokens)
        for cs, whole in pieces_now:
            whole.wait()
            weights = jnp.concatenate([in_v[i, cs, :] for i in range(draws)], axis=1)
            term_in = jnp.dot(act_v[rs, cs], weights, preferred_element_type=jnp.float32)
            weights = out_v[:, :, cs].reshape(draws * k_out, cs.stop - cs.start)
            term_out = lax.dot_general(
                grad_v[rs, cs], weights, (((1,), (1,)), ((), ())), preferred_element_type=jnp.float32
            )
            sums = (term_in, term_out) if sums is None else (sums[0] + term_in, sums[1] + term_out)
        return sums

    def factors(sums):
        low_in = sums[0].astype(jnp.bfloat16)
        found = []
        for e in range(part_count):
            ts = slice(e * length, (e + 1) * length)
            lhs = jnp.concatenate([sums[1][ts, i * k_out:(i + 1) * k_out] for i in range(draws)], axis=0)
            rhs = jnp.concatenate([low_in[ts, i * k_in:(i + 1) * k_in] for i in range(draws)], axis=0)
            found.append((lhs.T.astype(jnp.bfloat16), rhs))
        return found

    def terms(found, which, p, into):
        for e, (lhs, rhs) in enumerate(found):
            lhs = jnp.where(which == 0, lhs[:k_half], lhs[k_half:])
            into[p, pl.ds(e, k_half, stride=part_count), :] = jnp.dot(lhs, rhs, preferred_element_type=jnp.float32)

    def remote(src, dst, ssem, rsem, section, dp):
        return pltpu.make_async_remote_copy(
            src_ref=src, dst_ref=dst, send_sem=ssem, recv_sem=rsem,
            device_id={"section": section, "dp": dp}, device_id_type=MESH,
        )

    def across(c, i):
        bit = 1
        while bit < chips:
            if i & bit:
                c = c + bit * (1 - 2 * ((c // bit) % 2))
            bit *= 2
        return c

    k_chunk = k_half // chips
    rows = k_chunk * part_count
    turns = [2 * (m ^ m // 2) + b for m in range(1, chips // 2) for b in (0, 1)] + [1]

    def chunk(c):
        return pl.ds(pl.multiple_of(c * rows, rows), rows)

    def swap(p):
        return remote(theirs.at[p], arrived.at[p], load_sem.at[0], pair_sem.at[p], partner, d)

    def scatter(p):
        for slot, i in enumerate(turns):
            to = across(chip, i)
            ks = chunk(to)
            mine[p, ks, :] = mine[p, ks, :] + arrived[p, ks, :]
            remote(mine.at[p, ks], pieces.at[p, slot], load_sem.at[4], recv_sem.at[p], 2 * to + core, d).start()

    sums = []
    for p in range(parts):
        late = p == parts - 1
        early = spans[p][:TURN] if late else spans[p]
        total = project(p, early, None)
        if late:
            pl.semaphore_wait(barrier, n * groups)
            for o in range(p):
                swap(o).start()
            total = project(p, spans[p][TURN:], total)
        found = factors(total)
        terms(found, 1 - core, p, theirs)
        if late:
            swap(p).start()
            for o in range(p):
                swap(o).wait_recv()
                scatter(o)
        terms(found, core, p, mine)
    swap(parts - 1).wait_recv()
    scatter(parts - 1)
    hold = pltpu.make_async_copy(earlier, held, held_sem)
    hold.start()

    per_group = n // groups
    q = core * chips + chip
    own_slot = q % per_group
    home = q // per_group
    at_home = home == d

    cross = jnp.logical_not(at_home)
    direct = jnp.logical_and(chip == 0, d == 0)
    twice = jnp.logical_and(home == 0, jnp.logical_not(direct))

    def gather(p):
        ps = pl.ds(p * rows, rows)

        def col_copy(to):
            return remote(own.at[ps], cols.at[own_slot, d, ps], load_sem.at[1], col_recv.at[own_slot], to, home)

        for i in range(chips):
            to = jnp.where(core == 0, i, chips - 1 - i)
            col_copy(jnp.where(jnp.logical_and(at_home, chip == to), partner, 2 * to + core)).start()
            if i == 1:

                @pl.when(twice)
                def _():
                    remote(
                        own.at[ps], cols.at[own_slot, d, ps], load_sem.at[5], col_recv.at[own_slot], 1 - core, home
                    ).start()

        @pl.when(at_home)
        def _():
            cols[own_slot, d, ps] = own[ps]

        for g in range(groups):
            here = jnp.logical_and(q == s, d == g)

            @pl.when(jnp.logical_and(home != g, jnp.logical_not(here)))
            def _():
                remote(own.at[ps], row.at[d, ps], row_send.at[g], row_recv.at[d], q, g).start()

            @pl.when(jnp.logical_and(home != g, here))
            def _():
                row[d, ps] = own[ps]

    for p in range(parts):
        ks = chunk(chip)
        total = mine[p, ks, :] + arrived[p, ks, :]
        remote(pieces.at[p], pieces.at[p], load_sem.at[4], recv_sem.at[p], partner, d).wait_recv()
        for i in range(chips - 1):
            total = total + pieces[p, i]
        own[p * rows:(p + 1) * rows, :] = total
        gather(p)

    def rows_of(ref, k):
        starts = [p * rows + k * part_count for p in range(parts)]
        return jnp.concatenate([ref[g, at:at + part_count] for g in range(groups) for at in starts], axis=0)

    def forward(j, lo, size, sem):
        ref = cols.at[j, pl.ds(lo, size)]
        return remote(ref, ref, load_sem.at[sem], col_recv.at[j], partner, d)

    passes = jnp.logical_and(d * per_group // chips == core, jnp.logical_not(direct))
    for i in range(per_group):
        j = across(chip, i) % per_group
        mixed = d * per_group + j == q

        @pl.when(jnp.logical_not(mixed))
        def _():
            forward(j, 0, groups, 2).wait_recv()

            @pl.when(passes)
            def _():
                forward(j, 0, groups, 2).start()

        @pl.when(mixed)
        def _():
            forward(j, 0, groups - 1, 3).wait_recv()
            for g in range(groups):

                @pl.when(jnp.logical_and(passes, d != g))
                def _():
                    forward(j, g, 1, 3).start()

        for k in range(k_chunk):
            hi, lo = split(rows_of(cols.at[j], k))
            at = pl.multiple_of((j * k_chunk + k) * LANES, LANES)
            right[:, pl.ds(at, LANES)] = jnp.concatenate([hi, hi, lo], axis=0)

    for g in range(groups):

        @pl.when(jnp.logical_and(s // per_group != d, jnp.logical_or(q != s, d != g)))
        def _():
            remote(own, row.at[g], row_send.at[g], row_recv.at[g], q, d).wait_recv()

    @pl.when(s // per_group == d)
    def _():
        row[...] = cols[s % per_group]

    for k in range(k_chunk):
        hi, lo = split(rows_of(row, k) * scale)
        left[:, k * LANES:(k + 1) * LANES] = jnp.concatenate([hi, lo, hi], axis=0)

    hold.wait()
    remote(theirs, theirs, load_sem.at[0], recv_sem.at[0], partner, d).wait_send()
    remote(pieces, pieces, load_sem.at[4], recv_sem.at[0], partner, d).wait_send()
    remote(arrived, arrived, load_sem.at[1], recv_sem.at[0], partner, d).wait_send()
    for g in range(groups):

        @pl.when(jnp.logical_and(home != g, jnp.logical_or(q != s, d != g)))
        def _():
            remote(own, row.at[d], row_send.at[g], row_recv.at[d], q, g).wait_send()

    def forwarded(count, sem):
        ref = cols.at[pl.ds(0, count)]
        remote(ref, ref, load_sem.at[sem], recv_sem.at[0], partner, d).wait_send()

    @pl.when(twice)
    def _():
        remote(own, own, load_sem.at[5], recv_sem.at[0], partner, d).wait_send()

    @pl.when(jnp.logical_and(passes, at_home))
    def _():
        forwarded(per_group - 1, 2)
        forward(0, 0, groups - 1, 3).wait_send()

    @pl.when(jnp.logical_and(passes, cross))
    def _():
        forwarded(per_group, 2)


def gram_kernel(left, right, earlier, out, tile_v, sem):
    lhs = left[...].T
    at = 0
    for share in TILES:
        height = earlier.shape[0] * share // sum(TILES)
        rs = slice(at, at + height)
        tile_v[rs, :] = earlier[rs, :] + jnp.dot(lhs[rs], right[...], preferred_element_type=jnp.float32)
        pltpu.make_async_copy(tile_v.at[rs], out.at[rs], sem).start()
        at += height
    pltpu.make_async_copy(tile_v, out, sem).wait()


def per_device(activations, out_grads, proj_in, proj_out, earlier_gram):
    n = lax.axis_size("section")
    groups = lax.axis_size("dp")
    _, count, length, width = activations.shape
    _, draws, _, k_in = proj_in.shape
    k_out = proj_out.shape[2]
    tokens = count * length
    examples = count * groups
    scale = 1.0 / (length * n * draws) / examples
    row_width, col_width = earlier_gram.shape
    chips = n // 2
    k_half = k_out // 2
    k_chunk = k_half // chips
    per_group = n // groups
    parts = len(PIECES)
    half_rows = k_half * (count // parts)
    rows = half_rows // chips
    any_spec = pl.BlockSpec(memory_space=pl.ANY)
    vmem_spec = pl.BlockSpec(memory_space=pltpu.VMEM)
    f32, bf16 = jnp.float32, jnp.bfloat16
    dma = pltpu.SemaphoreType.DMA

    left, right, held = pl.pallas_call(
        functools.partial(feature_kernel, n, groups, count, scale),
        out_shape=(
            pltpu.VMEM((3 * examples, row_width), bf16),
            pltpu.VMEM((3 * examples, col_width), bf16),
            pltpu.VMEM((row_width, col_width), f32),
        ),
        in_specs=[any_spec] * 5,
        out_specs=(vmem_spec, vmem_spec, vmem_spec),
        scratch_shapes=[
            pltpu.VMEM((tokens, width), bf16),
            pltpu.VMEM((tokens, width), bf16),
            pltpu.VMEM((draws, width, k_in), bf16),
            pltpu.VMEM((draws, k_out, width), bf16),
            pltpu.VMEM((parts, half_rows, k_in), f32),
            pltpu.VMEM((parts, half_rows, k_in), f32),
            pltpu.VMEM((parts, half_rows, k_in), f32),
            pltpu.VMEM((parts, chips - 1, rows, k_in), f32),
            pltpu.VMEM((parts * rows, k_in), f32),
            pltpu.VMEM((per_group, groups, parts * rows, k_in), f32),
            pltpu.VMEM((groups, parts * rows, k_in), f32),
            dma((max(6, sum(len(shares) for shares in PIECES)),)),
            dma((parts,)),
            dma((parts,)),
            dma((per_group,)),
            dma((groups,)),
            dma((groups,)),
            dma,
        ],
        compiler_params=pltpu.CompilerParams(
            collective_id=0, has_side_effects=True, vmem_limit_bytes=52 << 20
        ),
        name="features",
    )(
        activations.reshape(tokens, width),
        out_grads.reshape(tokens, width),
        proj_in[0],
        proj_out[0],
        earlier_gram,
    )
    return pl.pallas_call(
        gram_kernel,
        out_shape=jax.ShapeDtypeStruct((row_width, col_width), f32),
        in_specs=[vmem_spec, vmem_spec, vmem_spec],
        out_specs=any_spec,
        scratch_shapes=[pltpu.VMEM((row_width, col_width), f32), dma],
        compiler_params=pltpu.CompilerParams(vmem_limit_bytes=28 << 20),
        name="gram",
    )(left, right, held)


def solution(mesh):
    return jax.shard_map(
        per_device,
        mesh=mesh,
        in_specs=(
            P("section", "dp", None, None),
            P("section", "dp", None, None),
            P("section", None, None, None),
            P("section", None, None, None),
            P("section", "dp"),
        ),
        out_specs=P("section", "dp"),
        check_vma=False,
    )
```

```python
import functools
import math

import jax
import jax.numpy as jnp
from jax import lax
from jax.experimental import pallas as pl
from jax.experimental.pallas import tpu as pltpu
from jax.sharding import PartitionSpec as P

MESH = pl.DeviceIdType.MESH
LANES = 128
PIECES = ((2, 2, 2, 2), (2, 2, 2, 2))
FIRST = 2
TURN = 1
TILES = (1, 1, 2, 4, 4, 4, 4, 4, 4, 2, 1, 1)


def split(x):
    hi = x.astype(jnp.bfloat16)
    lo = (x - hi.astype(jnp.float32)).astype(jnp.bfloat16)
    return hi, lo


def feature_kernel(
    n, groups, count, scale,
    act, grad, p_in, p_out, earlier,
    left, right, held,
    act_v, grad_v, in_v, out_v,
    theirs, mine, arrived, pieces, own, cols, row,
    load_sem, pair_sem, recv_sem, col_recv, row_recv, held_sem,
):
    s = lax.axis_index("section")
    d = lax.axis_index("dp")
    chips = n // 2
    core = s % 2
    chip = s // 2
    partner = s + 1 - 2 * core

    draws, width, k_in = p_in.shape
    k_out = p_out.shape[1]
    tokens = act.shape[0]
    length = tokens // count

    parts = len(PIECES)
    part_count = count // parts
    part_tokens = part_count * length
    k_half = k_out // 2
    half_rows = k_half * part_count

    loads, spans = [], []
    for p, shares in enumerate(PIECES):
        rs = slice(p * part_tokens, (p + 1) * part_tokens)
        spans.append([])
        at = 0
        for share in shares:
            depth = width * share // sum(shares)
            cs = slice(at, at + depth)
            at += depth
            sem = load_sem.at[len(loads)]
            copies = []
            if p == 0:
                copies.append(pltpu.make_async_copy(p_in.at[:, cs], in_v.at[:, cs], sem))
                copies.append(pltpu.make_async_copy(p_out.at[:, :, cs], out_v.at[:, :, cs], sem))
            copies.append(pltpu.make_async_copy(act.at[rs, cs], act_v.at[rs, cs], sem))
            copies.append(pltpu.make_async_copy(grad.at[rs, cs], grad_v.at[rs, cs], sem))
            taken = depth * (2 * part_tokens + (draws * (k_in + k_out) if p == 0 else 0)) // width
            whole = pltpu.make_async_copy(act.at[pl.ds(0, taken)], act_v.at[pl.ds(0, taken)], sem)
            spans[p].append((cs, whole))
            loads.append(copies)

    def start(some):
        for copies in some:
            for copy in copies:
                copy.start()

    start(loads[:FIRST])
    barrier = pltpu.get_barrier_semaphore()
    for g in range(groups):
        for i in range(n):
            pl.semaphore_signal(barrier, inc=1, device_id={"section": i, "dp": g}, device_id_type=MESH)
    start(loads[FIRST:])

    def project(p, pieces_now, sums):
        rs = slice(p * part_tokens, (p + 1) * part_tokens)
        for cs, whole in pieces_now:
            whole.wait()
            weights = jnp.concatenate([in_v[i, cs, :] for i in range(draws)], axis=1)
            term_in = jnp.dot(act_v[rs, cs], weights, preferred_element_type=jnp.float32)
            weights = out_v[:, :, cs].reshape(draws * k_out, cs.stop - cs.start)
            term_out = lax.dot_general(
                grad_v[rs, cs], weights, (((1,), (1,)), ((), ())), preferred_element_type=jnp.float32
            )
            sums = (term_in, term_out) if sums is None else (sums[0] + term_in, sums[1] + term_out)
        return sums

    def factors(sums):
        low_in = sums[0].astype(jnp.bfloat16)
        found = []
        for e in range(part_count):
            ts = slice(e * length, (e + 1) * length)
            lhs = jnp.concatenate([sums[1][ts, i * k_out:(i + 1) * k_out] for i in range(draws)], axis=0)
            rhs = jnp.concatenate([low_in[ts, i * k_in:(i + 1) * k_in] for i in range(draws)], axis=0)
            found.append((lhs.T.astype(jnp.bfloat16), rhs))
        return found

    def terms(found, which, p, into):
        for e, (lhs, rhs) in enumerate(found):
            lhs = jnp.where(which == 0, lhs[:k_half], lhs[k_half:])
            into[p, pl.ds(e, k_half, stride=part_count), :] = jnp.dot(lhs, rhs, preferred_element_type=jnp.float32)

    def remote(src, dst, ssem, rsem, section, dp):
        return pltpu.make_async_remote_copy(
            src_ref=src, dst_ref=dst, send_sem=ssem, recv_sem=rsem,
            device_id={"section": section, "dp": dp}, device_id_type=MESH,
        )

    def across(c, i):
        bit = 1
        while bit < chips:
            if i & bit:
                c = c + bit * (1 - 2 * ((c // bit) % 2))
            bit *= 2
        return c

    k_chunk = k_half // chips
    rows = k_chunk * part_count
    turns = [2 * (m ^ m // 2) + b for m in range(1, chips // 2) for b in (0, 1)] + [1]

    def chunk(c):
        return pl.ds(pl.multiple_of(c * rows, rows), rows)

    def swap(p):
        return remote(theirs.at[p], arrived.at[p], load_sem.at[0], pair_sem.at[p], partner, d)

    def scatter(p):
        for slot, i in enumerate(turns):
            to = across(chip, i)
            ks = chunk(to)
            mine[p, ks, :] = mine[p, ks, :] + arrived[p, ks, :]
            remote(mine.at[p, ks], pieces.at[p, slot], load_sem.at[4], recv_sem.at[p], 2 * to + core, d).start()

    sums = []
    for p in range(parts):
        late = p == parts - 1
        early = spans[p][:TURN] if late else spans[p]
        total = project(p, early, None)
        if late:
            pl.semaphore_wait(barrier, n * groups)
            for o in range(p):
                swap(o).start()
            total = project(p, spans[p][TURN:], total)
        found = factors(total)
        terms(found, 1 - core, p, theirs)
        if late:
            swap(p).start()
            for o in range(p):
                swap(o).wait_recv()
                scatter(o)
        terms(found, core, p, mine)
    swap(parts - 1).wait_recv()
    scatter(parts - 1)
    hold = pltpu.make_async_copy(earlier, held, held_sem)
    hold.start()

    per_group = n // groups
    q = core * chips + chip
    own_slot = q % per_group
    home = q // per_group
    at_home = home == d

    cross = jnp.logical_not(at_home)
    direct = jnp.logical_and(chip == 0, d == 0)
    twice = jnp.logical_and(home == 0, jnp.logical_not(direct))

    def gather(p):
        ps = pl.ds(p * rows, rows)

        def col_copy(to):
            return remote(own.at[ps], cols.at[own_slot, d, ps], load_sem.at[1], col_recv.at[own_slot], to, home)

        for i in range(chips):
            to = jnp.where(core == 0, i, (i + chips // 2) % chips)
            col_copy(jnp.where(jnp.logical_and(at_home, chip == to), partner, 2 * to + core)).start()
            if i == 1:

                @pl.when(twice)
                def _():
                    remote(
                        own.at[ps], cols.at[own_slot, d, ps], load_sem.at[5], col_recv.at[own_slot], 1 - core, home
                    ).start()

        @pl.when(at_home)
        def _():
            cols[own_slot, d, ps] = own[ps]

        for g in range(groups):
            here = jnp.logical_and(q == s, d == g)

            @pl.when(jnp.logical_and(home != g, jnp.logical_not(here)))
            def _():
                remote(own.at[ps], row.at[d, ps], load_sem.at[6 + g], row_recv.at[d], q, g).start()

            @pl.when(jnp.logical_and(home != g, here))
            def _():
                row[d, ps] = own[ps]

    for p in range(parts):
        ks = chunk(chip)
        total = mine[p, ks, :] + arrived[p, ks, :]
        remote(pieces.at[p], pieces.at[p], load_sem.at[4], recv_sem.at[p], partner, d).wait_recv()
        for i in range(chips - 1):
            total = total + pieces[p, i]
        own[p * rows:(p + 1) * rows, :] = total
        gather(p)

    def rows_of(ref, k):
        starts = [p * rows + k * part_count for p in range(parts)]
        return jnp.concatenate([ref[g, at:at + part_count] for g in range(groups) for at in starts], axis=0)

    def forward(j, lo, size, sem):
        ref = cols.at[j, pl.ds(lo, size)]
        return remote(ref, ref, load_sem.at[sem], col_recv.at[j], partner, d)

    passes = jnp.logical_and(d * per_group // chips == core, jnp.logical_not(direct))
    for i in range(per_group):
        j = across(chip, i) % per_group
        mixed = d * per_group + j == q

        @pl.when(jnp.logical_not(mixed))
        def _():
            forward(j, 0, groups, 2).wait_recv()

            @pl.when(passes)
            def _():
                forward(j, 0, groups, 2).start()

        @pl.when(mixed)
        def _():
            forward(j, 0, groups - 1, 3).wait_recv()
            for g in range(groups):

                @pl.when(jnp.logical_and(passes, d != g))
                def _():
                    forward(j, g, 1, 3).start()

        for k in range(k_chunk):
            hi, lo = split(rows_of(cols.at[j], k))
            at = pl.multiple_of((j * k_chunk + k) * LANES, LANES)
            right[:, pl.ds(at, LANES)] = jnp.concatenate([hi, hi, lo], axis=0)

    for g in range(groups):

        @pl.when(jnp.logical_and(s // per_group != d, jnp.logical_or(q != s, d != g)))
        def _():
            remote(own, row.at[g], load_sem.at[6 + g], row_recv.at[g], q, d).wait_recv()

    @pl.when(s // per_group == d)
    def _():
        row[...] = cols[s % per_group]

    for k in range(k_chunk):
        hi, lo = split(rows_of(row, k) * scale)
        left[:, k * LANES:(k + 1) * LANES] = jnp.concatenate([hi, lo, hi], axis=0)

    hold.wait()
    remote(theirs, theirs, load_sem.at[0], recv_sem.at[0], partner, d).wait_send()
    remote(pieces, pieces, load_sem.at[4], recv_sem.at[0], partner, d).wait_send()
    remote(arrived, arrived, load_sem.at[1], recv_sem.at[0], partner, d).wait_send()
    for g in range(groups):

        @pl.when(jnp.logical_and(home != g, jnp.logical_or(q != s, d != g)))
        def _():
            remote(own, row.at[d], load_sem.at[6 + g], row_recv.at[d], q, g).wait_send()

    def forwarded(count, sem):
        ref = cols.at[pl.ds(0, count)]
        remote(ref, ref, load_sem.at[sem], recv_sem.at[0], partner, d).wait_send()

    @pl.when(twice)
    def _():
        remote(own, own, load_sem.at[5], recv_sem.at[0], partner, d).wait_send()

    @pl.when(jnp.logical_and(passes, at_home))
    def _():
        forwarded(per_group - 1, 2)
        forward(0, 0, groups - 1, 3).wait_send()

    @pl.when(jnp.logical_and(passes, cross))
    def _():
        forwarded(per_group, 2)


def gram_kernel(left, right, earlier, out, tile_v, sem):
    lhs = left[...].T
    at = 0
    for share in TILES:
        height = earlier.shape[0] * share // sum(TILES)
        rs = slice(at, at + height)
        tile_v[rs, :] = earlier[rs, :] + jnp.dot(lhs[rs], right[...], preferred_element_type=jnp.float32)
        pltpu.make_async_copy(tile_v.at[rs], out.at[rs], sem).start()
        at += height
    pltpu.make_async_copy(tile_v, out, sem).wait()


def per_device(activations, out_grads, proj_in, proj_out, earlier_gram):
    n = lax.axis_size("section")
    groups = lax.axis_size("dp")
    _, count, length, width = activations.shape
    _, draws, _, k_in = proj_in.shape
    k_out = proj_out.shape[2]
    tokens = count * length
    examples = count * groups
    scale = 1.0 / (length * n * draws) / examples
    row_width, col_width = earlier_gram.shape
    chips = n // 2
    k_half = k_out // 2
    k_chunk = k_half // chips
    per_group = n // groups
    parts = len(PIECES)
    half_rows = k_half * (count // parts)
    rows = half_rows // chips
    any_spec = pl.BlockSpec(memory_space=pl.ANY)
    vmem_spec = pl.BlockSpec(memory_space=pltpu.VMEM)
    f32, bf16 = jnp.float32, jnp.bfloat16
    dma = pltpu.SemaphoreType.DMA

    left, right, held = pl.pallas_call(
        functools.partial(feature_kernel, n, groups, count, scale),
        out_shape=(
            pltpu.VMEM((3 * examples, row_width), bf16),
            pltpu.VMEM((3 * examples, col_width), bf16),
            pltpu.VMEM((row_width, col_width), f32),
        ),
        in_specs=[any_spec] * 5,
        out_specs=(vmem_spec, vmem_spec, vmem_spec),
        scratch_shapes=[
            pltpu.VMEM((tokens, width), bf16),
            pltpu.VMEM((tokens, width), bf16),
            pltpu.VMEM((draws, width, k_in), bf16),
            pltpu.VMEM((draws, k_out, width), bf16),
            pltpu.VMEM((parts, half_rows, k_in), f32),
            pltpu.VMEM((parts, half_rows, k_in), f32),
            pltpu.VMEM((parts, half_rows, k_in), f32),
            pltpu.VMEM((parts, chips - 1, rows, k_in), f32),
            pltpu.VMEM((parts * rows, k_in), f32),
            pltpu.VMEM((per_group, groups, parts * rows, k_in), f32),
            pltpu.VMEM((groups, parts * rows, k_in), f32),
            dma((max(6 + groups, sum(len(shares) for shares in PIECES)),)),
            dma((parts,)),
            dma((parts,)),
            dma((per_group,)),
            dma((groups,)),
            dma,
        ],
        compiler_params=pltpu.CompilerParams(
            collective_id=0, has_side_effects=True, vmem_limit_bytes=52 << 20
        ),
        name="features",
    )(
        activations.reshape(tokens, width),
        out_grads.reshape(tokens, width),
        proj_in[0],
        proj_out[0],
        earlier_gram,
    )
    return pl.pallas_call(
        gram_kernel,
        out_shape=jax.ShapeDtypeStruct((row_width, col_width), f32),
        in_specs=[vmem_spec, vmem_spec, vmem_spec],
        out_specs=any_spec,
        scratch_shapes=[pltpu.VMEM((row_width, col_width), f32), dma],
        compiler_params=pltpu.CompilerParams(vmem_limit_bytes=28 << 20),
        name="gram",
    )(left, right, held)


def solution(mesh):
    return jax.shard_map(
        per_device,
        mesh=mesh,
        in_specs=(
            P("section", "dp", None, None),
            P("section", "dp", None, None),
            P("section", None, None, None),
            P("section", None, None, None),
            P("section", "dp"),
        ),
        out_specs=P("section", "dp"),
        check_vma=False,
    )
```
